768 devices in a mesh: row: 24 (over z, x_hi), col: 32 (over x_lo, y, core).
Axes of the slice: x: 4 (x_hi: 2, x_lo: 2; x = x_hi * 2 + x_lo), y: 8, z: 12, core: 2. Of those that a mesh axis runs over, the one named last changes fastest.
Arguments:
- object_field: float32 [2, 6144, 8192], P(None, 'row', 'col'), may hold values from -4 to 4
- probe_field: float32 [2, 256, 256], replicated, may hold values from -6 to 6
- measured: float32 [96, 8192, 256], P('row', 'col'), may hold values from 0.1 to 4
- positions: int32 [96, 64], P('row', 'col'), may hold values from 0 to 160
Outputs:
- new_object: float32 [2, 6144, 8192], P(None, 'row', 'col')
- new_probe: float32 [2, 256, 256], replicated
The draws below stay inside these ranges and needn't reach their ends.
Inputs may be any that keep to these rules, and one draw needn't show every extreme that they name: `positions`: each entry is a pixel offset of a window's top-left corner within its device's tile.
All inputs are finite; a program needn't handle non-finite values.
Results may differ from the reference program's by a relative error of at most 0.0003.
Values sent between devices are 32-bit elements; how exact they have to be, the bound alone decides.
A program may use at most 32 MiB of HBM per device.

```python
import math
import jax
import jax.numpy as jnp
from jax import lax

F = 256
TILE = 256
FR_DEV = 4
HALO = 160
NY = 6144
NX = 8192
N_ROW = 24
N_COL = 32


def place_ends(result, rng, smallest, top_value):
    dims = result.shape
    index_at = [jax.random.randint(jax.random.fold_in(rng, axis), (), 0, dims[axis]) for axis in range(len(dims))]
    result = result.at[tuple(index_at)].set(smallest)
    longest = dims.index(max(dims))
    index_at[longest] = (index_at[longest] + 1) % dims[longest]
    return result.at[tuple(index_at)].set(top_value)


def shard_levels(rng, shape, cuts, low, high):
    def one(axis_at, shards_of):
        steps = jax.random.uniform(jax.random.fold_in(jax.random.fold_in(rng, 6), axis_at), (shards_of,), jnp.float32, low / len(cuts), high / len(cuts))
        return jnp.repeat(jnp.exp(steps), shape[axis_at] // shards_of).reshape((-1,) + (1,) * (len(shape) - axis_at - 1))

    level = one(*cuts[0])
    for cut in cuts[1:]:
        level = level * one(*cut)
    return level


def normal_values(stream_key, extent, scale, reach, cuts=(), held_as=jnp.bfloat16):
    drawn = jax.random.normal(stream_key, extent, jnp.float32) * scale
    if len(cuts) > 0:
        drawn = shard_levels(stream_key, extent, cuts, -0.22, 0.18) * drawn
    return jnp.clip(drawn, min=-reach, max=reach).astype(held_as)


def setup_inputs(seed: int = 0) -> dict:
    seeds = jax.random.split(jax.random.key(seed), 5)
    return {
        "object_field": normal_values(seeds[0], (2, NY, NX), 0.7, 4.0, ((1, 24), (2, 32)), jnp.float32),
        "probe_field": normal_values(seeds[1], (2, F, F), 1.0, 6.0, (), jnp.float32),
        "measured": jnp.clip(jnp.exp(math.log(4.0) - 3.6888794 * jax.random.uniform(seeds[2], (N_ROW * FR_DEV, N_COL * F, F), jnp.float32) ** shard_levels(seeds[2], (N_ROW * FR_DEV, N_COL * F, F), ((0, 24), (1, 32)), -0.2, 0.2)), 0.1, 4.0),
        "positions": place_ends(jax.random.randint(seeds[3], (N_ROW * FR_DEV, N_COL * 2), 0, HALO + TILE - F + 1), jax.random.fold_in(seeds[3], 1), 0, HALO + TILE - F).astype(jnp.int32),
    }


def reference(object_field, probe_field, measured, positions):
    padded = jnp.pad(object_field, ((0, 0), (0, HALO), (0, HALO)))
    probe_cplx = lax.complex(probe_field[0], probe_field[1])
    per_row = N_COL * FR_DEV

    def one_frame(carry, index):
        grad_acc, probe_acc, inten_acc = carry
        row_dev = index // per_row
        rest = index % per_row
        col_dev = rest // FR_DEV
        frame = rest % FR_DEV
        line = row_dev * FR_DEV + frame
        row_off = positions[line, 2 * col_dev]
        col_off = positions[line, 2 * col_dev + 1]
        top = (row_dev * TILE + row_off).astype(jnp.int32)
        left = (col_dev * TILE + col_off).astype(jnp.int32)
        zero = jnp.int32(0)
        window = lax.dynamic_slice(padded, (zero, top, left), (2, F, F))
        ampl = lax.dynamic_slice(measured, (line.astype(jnp.int32), (col_dev * F).astype(jnp.int32), zero), (1, F, F))[0]
        wind_c = lax.complex(window[0], window[1])
        spectrum = jnp.fft.fft2(probe_cplx * wind_c, norm="ortho")
        factor = ampl / jnp.maximum(jnp.abs(spectrum), 0.5) - 1.0
        change = jnp.fft.ifft2(factor * spectrum, norm="ortho")
        obj_grad = jnp.conj(probe_cplx) * change
        pro_grad = jnp.conj(wind_c) * change
        piece = jnp.stack([jnp.real(obj_grad), jnp.imag(obj_grad)])
        old = lax.dynamic_slice(grad_acc, (zero, top, left), (2, F, F))
        grad_acc = lax.dynamic_update_slice(grad_acc, old + piece, (zero, top, left))
        probe_acc = probe_acc + jnp.stack([jnp.real(pro_grad), jnp.imag(pro_grad)])
        inten_acc = inten_acc + window[0] * window[0] + window[1] * window[1]
        return (grad_acc, probe_acc, inten_acc), None

    init = (jnp.zeros(padded.shape, jnp.float32), jnp.zeros((2, F, F), jnp.float32), jnp.zeros((F, F), jnp.float32))
    count = N_ROW * N_COL * FR_DEV
    (grad_acc, probe_acc, inten_acc), _ = lax.scan(one_frame, init, jnp.arange(count, dtype=jnp.int32))
    grad_obj = grad_acc[:, :NY, :NX]
    largest = jnp.max(probe_field[0] ** 2 + probe_field[1] ** 2)
    new_object = object_field + grad_obj / largest
    new_probe = probe_field + probe_acc / (inten_acc + 1.0)
    return new_object, new_probe
```

```python
import functools
import math

import jax
import jax.numpy as jnp
import numpy as np
from jax import lax
from jax.experimental import pallas as pl
from jax.experimental.pallas import tpu as pltpu
from jax.sharding import PartitionSpec as P

MESH = pl.DeviceIdType.MESH
DMA = pltpu.SemaphoreType.DMA
F = 256
HALF = 128
HALO = 160
EXT = F + HALO
CHUNKS = 5
TALL = F + 8
WIDE = F + 128
DEEP = EXT + 8
STEP = HALO // CHUNKS
NX, NY, NZ = 4, 8, 12
F32 = jnp.float32
BF16 = jnp.bfloat16
VMEM_SPEC = pl.BlockSpec(memory_space=pltpu.VMEM)
ANY_SPEC = pl.BlockSpec(memory_space=pl.ANY)


class Place:
    def __init__(self):
        self.row = lax.axis_index("row")
        self.col = lax.axis_index("col")
        self.rows = lax.axis_size("row")
        self.cols = lax.axis_size("col")
        self.z = lax.div(self.row, 2)
        self.x = 2 * lax.rem(self.row, 2) + lax.div(self.col, 16)
        self.y = lax.rem(lax.div(self.col, 2), NY)
        self.core = lax.rem(self.col, 2)

    def at(self, x, y, z, core):
        return (2 * z + lax.div(x, 2), 16 * lax.rem(x, 2) + 2 * y + core)

    def partner(self):
        return self.at(self.x, self.y, self.z, 1 - self.core)

    def along_x(self, i):
        return self.at(lax.rem(self.x + i, NX), self.y, self.z, self.core)

    def along_y(self, i):
        return self.at(self.x, lax.rem(self.y + i, NY), self.z, self.core)

    def along_z(self, i):
        return self.at(self.x, self.y, lax.rem(self.z + i, NZ), self.core)

    def up(self):
        return (lax.rem(self.row + self.rows - 1, self.rows), self.col)

    def down(self):
        return (lax.rem(self.row + 1, self.rows), self.col)

    def left(self):
        return (self.row, lax.rem(self.col + self.cols - 1, self.cols))

    def right(self):
        return (self.row, lax.rem(self.col + 1, self.cols))


def meet(devices):
    barrier = pltpu.get_barrier_semaphore()
    for device in devices:
        pl.semaphore_signal(barrier, inc=1, device_id=device, device_id_type=MESH)
    pl.semaphore_wait(barrier, len(devices))


def send(src, dst, send_sem, recv_sem, device):
    copy = pltpu.make_async_remote_copy(
        src_ref=src,
        dst_ref=dst,
        send_sem=send_sem,
        recv_sem=recv_sem,
        device_id=device,
        device_id_type=MESH,
    )
    copy.start()
    return copy


def far_first(count):
    order = []
    for d in range(count // 2, 0, -1):
        order.append(d)
        if count - d != d:
            order.append(count - d)
    return order


def halo_kernel(obj, right, below, corner, row_s, row_r, col_s, col_r, cor_s, cor_r):
    place = Place()
    up, left = place.up(), place.left()
    meet((up, place.down(), left, place.right()))
    rows = []
    for k in range(CHUNKS):
        part = (slice(None), pl.ds(k * STEP, STEP))
        rows.append(send(obj.at[part], below.at[part], row_s.at[k], row_r.at[k], up))
    side = send(obj, right, col_s, col_r, left)
    corners = []
    for k in range(CHUNKS):
        part = (slice(None), pl.ds(k * STEP, STEP))
        rows[k].wait_recv()
        corners.append(
            send(below.at[part], corner.at[part], cor_s.at[k], cor_r.at[k], left)
        )
    side.wait()
    for k in range(CHUNKS):
        rows[k].wait_send()
        corners[k].wait()


def halo_exchange(obj):
    rows = jax.ShapeDtypeStruct((2, HALO, F), F32)
    return pl.pallas_call(
        halo_kernel,
        name="halo",
        out_shape=(jax.ShapeDtypeStruct((2, F, F), F32), rows, rows),
        in_specs=[VMEM_SPEC],
        out_specs=(VMEM_SPEC, VMEM_SPEC, VMEM_SPEC),
        scratch_shapes=[
            DMA((CHUNKS,)),
            DMA((CHUNKS,)),
            DMA,
            DMA,
            DMA((CHUNKS,)),
            DMA((CHUNKS,)),
        ],
        compiler_params=pltpu.CompilerParams(collective_id=0, has_side_effects=True),
    )(obj)


def split(x):
    high = x.astype(BF16)
    return high, (x - high.astype(F32)).astype(BF16)


def dot(a, b):
    return jnp.dot(a, b, preferred_element_type=F32)


def left_mult(high, low, x):
    x_high, x_low = split(x)
    return dot(high, x_high) + (dot(high, x_low) + dot(low, x_high))


def right_mult(x, high, low):
    x_high, x_low = split(x)
    return dot(x_high, high) + (dot(x_low, high) + dot(x_high, low))


def tables():
    k = np.arange(HALF)
    angle = 2.0 * math.pi / HALF * (np.outer(k, k) % HALF)
    cos, sin = np.cos(angle) / 16.0, np.sin(angle) / 16.0
    t1 = np.block([[cos, sin], [-sin, cos]]).astype(np.float32)
    stack = []
    for t in (t1, t1.T):
        high = t.astype(jnp.bfloat16)
        stack += [high, (t - high.astype(np.float32)).astype(jnp.bfloat16)]
    order = np.zeros((F, F), np.float32)
    for v in range(HALF):
        order[2 * v, v] = 1.0
        order[2 * v + 1, HALF + v] = 1.0
    stack.append(order.astype(jnp.bfloat16))
    turn = 2.0 * math.pi / F * k
    down = [np.broadcast_to(f(turn)[:, None], (HALF, HALF)) for f in (np.cos, np.sin)]
    across = [np.broadcast_to(f(turn)[None, :], (8, HALF)) for f in (np.cos, np.sin)]
    twiddle = np.concatenate(down + across, 0).astype(np.float32)
    return np.stack(stack), twiddle


def frame_kernel(
    pos, obj, right, below, corner, probe, measured, mats, twiddle,
    grad, sums, probe_tiles, ext, acc, scale, thin, sems,
):
    frame = pl.program_id(0)
    place = Place()

    @pl.when(frame == 0)
    def _():
        copies = [
            pltpu.make_async_copy(src, ext.at[:, pl.ds(r, n), pl.ds(c, F)], sems.at[i])
            for i, (src, r, n, c) in enumerate(
                ((obj, 0, F, 0), (right, 0, F, F), (below, F, HALO, 0), (corner, F, HALO, F))
            )
        ]
        for copy in copies:
            copy.start()
        grad[...] = jnp.zeros_like(grad)
        acc[...] = jnp.zeros_like(acc)
        p_re, p_im = probe[0], probe[1]
        power = jnp.max(p_re * p_re + p_im * p_im, axis=0, keepdims=True)
        top = jnp.max(power, axis=1, keepdims=True)
        scale[...] = 1.0 / jnp.broadcast_to(top, scale.shape)
        for t in range(32):
            for h in range(2):
                for c in range(2):
                    probe_tiles[2 * t + h, 8 * c : 8 * c + 8] = probe[
                        c, 8 * t : 8 * t + 8, HALF * h : HALF * h + HALF
                    ]
        for copy in copies:
            copy.wait()

        @pl.when(place.col == place.cols - 1)
        def _():
            ext[:, :, F:] = jnp.zeros((2, DEEP, F), F32)

        @pl.when(place.row == place.rows - 1)
        def _():
            ext[:, F:, :] = jnp.zeros((2, DEEP - F, 2 * F), F32)

    dy, dx = pos[frame, 0], pos[frame, 1]
    r_dy, r_dx = lax.rem(dy, 8), lax.rem(dx, HALF)
    rows = pl.ds(pl.multiple_of(dy - r_dy, 8), TALL)
    lanes = pl.ds(pl.multiple_of(dx - r_dx, HALF), WIDE)
    back_dy, back_dx = lax.rem(TALL - r_dy, TALL), lax.rem(WIDE - r_dx, WIDE)

    def window(c):
        return pltpu.roll(pltpu.roll(ext[c, rows, lanes], back_dx, 1)[:, :F], back_dy, 0)[:F]

    o_re, o_im = window(0), window(1)
    p_re, p_im = probe[0], probe[1]
    t1_high, t1_low, t2_high, t2_low, order = (mats[i] for i in range(5))
    down_c = jnp.concatenate([twiddle[:HALF]] * 2, 1)
    down_s = jnp.concatenate([twiddle[HALF:F]] * 2, 1)
    over_c, over_s = twiddle[F : F + 1], twiddle[F + 8 : F + 9]

    for h in range(2):
        thin[h] = measured[0, :, HALF * h : HALF * h + HALF]
    even = [thin[h, pl.ds(0, HALF, 2), :] for h in range(2)]
    odd = [thin[h, pl.ds(1, HALF, 2), :] for h in range(2)]
    sorted_rows = jnp.concatenate([jnp.concatenate(even, 1), jnp.concatenate(odd, 1)], 0)
    m_high, m_low = split(sorted_rows)
    ampl = dot(m_high, order) + dot(m_low, order)

    w_re = p_re * o_re - p_im * o_im
    w_im = p_re * o_im + p_im * o_re
    d_re, d_im = w_re[:HALF] - w_re[HALF:], w_im[:HALF] - w_im[HALF:]
    a = jnp.concatenate([w_re[:HALF] + w_re[HALF:], w_im[:HALF] + w_im[HALF:]], 0)
    b = jnp.concatenate([d_re * down_c + d_im * down_s, d_im * down_c - d_re * down_s], 0)
    y_even, y_odd = left_mult(t1_high, t1_low, a), left_mult(t1_high, t1_low, b)
    x_re = jnp.concatenate([y_even[:HALF], y_odd[:HALF]], 0)
    x_im = jnp.concatenate([y_even[HALF:], y_odd[HALF:]], 0)
    d_re, d_im = x_re[:, :HALF] - x_re[:, HALF:], x_im[:, :HALF] - x_im[:, HALF:]
    a = jnp.concatenate([x_re[:, :HALF] + x_re[:, HALF:], x_im[:, :HALF] + x_im[:, HALF:]], 1)
    b = jnp.concatenate([d_re * over_c + d_im * over_s, d_im * over_c - d_re * over_s], 1)

    def fit(x, target):
        re, im = x[:, :HALF], x[:, HALF:]
        factor = target * jnp.minimum(lax.rsqrt(re * re + im * im), 2.0) - 1.0
        return jnp.concatenate([re * factor, im * factor], 1)

    s_even = fit(right_mult(a, t2_high, t2_low), ampl[:, :HALF])
    s_odd = fit(right_mult(b, t2_high, t2_low), ampl[:, HALF:])
    e, o = right_mult(s_even, t1_high, t1_low), right_mult(s_odd, t1_high, t1_low)
    e_re, e_im, o_re2, o_im2 = e[:, :HALF], e[:, HALF:], o[:, :HALF], o[:, HALF:]
    q_re, q_im = o_re2 * over_c - o_im2 * over_s, o_im2 * over_c + o_re2 * over_s
    x_re = jnp.concatenate([e_re + q_re, e_re - q_re], 1)
    x_im = jnp.concatenate([e_im + q_im, e_im - q_im], 1)
    e = left_mult(t2_high, t2_low, jnp.concatenate([x_re[:HALF], x_im[:HALF]], 0))
    o = left_mult(t2_high, t2_low, jnp.concatenate([x_re[HALF:], x_im[HALF:]], 0))
    e_re, e_im, o_re2, o_im2 = e[:HALF], e[HALF:], o[:HALF], o[HALF:]
    q_re, q_im = o_re2 * down_c - o_im2 * down_s, o_im2 * down_c + o_re2 * down_s
    c_re = jnp.concatenate([e_re + q_re, e_re - q_re], 0)
    c_im = jnp.concatenate([e_im + q_im, e_im - q_im], 0)

    acc[0] += o_re * c_re + o_im * c_im
    acc[1] += o_re * c_im - o_im * c_re
    acc[2] += o_re * o_re + o_im * o_im
    inverse = scale[0:1, 0:1]
    blank_rows, blank_lanes = jnp.zeros((TALL - F, F), F32), jnp.zeros((TALL, WIDE - F), F32)
    for c, g in ((0, p_re * c_re + p_im * c_im), (1, p_re * c_im - p_im * c_re)):
        moved = pltpu.roll(jnp.concatenate([g * inverse, blank_rows], 0), r_dy, 0)
        moved = pltpu.roll(jnp.concatenate([moved, blank_lanes], 1), r_dx, 1)
        grad[c, rows, lanes] += moved

    @pl.when(frame == pl.num_programs(0) - 1)
    def _():
        for t in range(32):
            for h in range(2):
                for c in range(3):
                    sums[2 * t + h, 8 * c : 8 * c + 8] = acc[
                        c, 8 * t : 8 * t + 8, HALF * h : HALF * h + HALF
                    ]


def frame_step(positions, obj, right, below, corner, probe, measured):
    mats, twiddle = tables()

    def whole(shape):
        return pl.BlockSpec(shape, lambda f: (0,) * len(shape))

    return pl.pallas_call(
        frame_kernel,
        name="frames",
        grid=(measured.shape[0],),
        out_shape=(
            jax.ShapeDtypeStruct((2, DEEP, 2 * F), F32),
            jax.ShapeDtypeStruct((64, 24, HALF), F32),
            jax.ShapeDtypeStruct((64, 16, HALF), F32),
        ),
        in_specs=[
            pl.BlockSpec(memory_space=pltpu.SMEM),
            ANY_SPEC,
            ANY_SPEC,
            ANY_SPEC,
            ANY_SPEC,
            whole((2, F, F)),
            pl.BlockSpec((1, F, F), lambda f: (f, 0, 0)),
            whole((5, F, F)),
            whole((F + 16, HALF)),
        ],
        out_specs=(whole((2, DEEP, 2 * F)), whole((64, 24, HALF)), whole((64, 16, HALF))),
        scratch_shapes=[
            pltpu.VMEM((2, DEEP, 2 * F), F32),
            pltpu.VMEM((3, F, F), F32),
            pltpu.VMEM((8, HALF), F32),
            pltpu.VMEM((2, F, HALF), F32),
            DMA((4,)),
        ],
    )(positions, obj, right, below, corner, probe, measured, jnp.asarray(mats), jnp.asarray(twiddle))


def reduce_kernel(
    grad, sums, probe_tiles, obj, new_obj, new_probe,
    main, side, below, bottom, core_in, half, y_in, y_sum, x_in, x_sum, z_in, tiles,
    local_s, core_s, core_r, y_s, y_r, x_s, x_r, z_s, z_r, xg_s, xg_r, yg_s, yg_r, cg_s, cg_r,
    side_s, side_r, bot_s, bot_r,
):
    place = Place()
    core, x, y, z = place.core, place.x, place.y, place.z
    partner, right, down = place.partner(), place.right(), place.down()
    peers = [partner, right, place.left(), down, place.up()]
    peers += [place.along_x(i) for i in range(1, NX)]
    peers += [place.along_y(i) for i in range(1, NY)]
    peers += [place.along_z(i) for i in range(1, NZ)]
    meet(peers)

    fetch = pltpu.make_async_copy(grad.at[:, pl.ds(0, EXT), pl.ds(0, F)], main, local_s)
    fetch.start()
    first = send(sums.at[pl.ds(32 * (1 - core), 32)], core_in, core_s, core_r, partner)
    first.wait()
    half[...] = sums[pl.ds(32 * core, 32)] + core_in[...]

    y_out = []
    for i in far_first(NY):
        there = lax.rem(y + i, NY)
        y_out.append(
            send(half.at[pl.ds(4 * there, 4)], y_in.at[i - 1], y_s.at[i], y_r.at[i], place.along_y(i))
        )
    for copy in y_out:
        copy.wait()
    total = half[pl.ds(4 * y, 4)]
    for i in range(NY - 1):
        total = total + y_in[i]
    y_sum[...] = total

    x_out = []
    for i in far_first(NX):
        there = lax.rem(x + i, NX)
        x_out.append(send(y_sum.at[there], x_in.at[i - 1], x_s.at[i], x_r.at[i], place.along_x(i)))
    side_out = []
    for k in range(CHUNKS + 1):
        part = (slice(None), pl.ds(F + k * STEP, STEP) if k < CHUNKS else pl.ds(0, F))
        src = grad.at[part + (pl.ds(F, F),)]
        side_out.append(send(src, side.at[part], side_s.at[k], side_r.at[k], right))
    for copy in x_out:
        copy.wait()
    x_sum[...] = ((y_sum[x] + x_in[0]) + x_in[1]) + x_in[2]

    z_out = []
    for i in far_first(NZ):
        z_out.append(send(x_sum, z_in.at[z], z_s.at[i], z_r.at[i], place.along_z(i)))
    z_in[z] = x_sum[...]

    fetch.wait()
    first_col = place.col == 0
    bottom_out = []
    for k in range(CHUNKS):
        side_out[k].wait()
        rows = pl.ds(F + k * STEP, STEP)
        extra = jnp.where(first_col, 0.0, side[:, rows, :])
        bottom[:, pl.ds(k * STEP, STEP), :] = main[:, rows, :] + extra
        part = (slice(None), pl.ds(k * STEP, STEP))
        bottom_out.append(send(bottom.at[part], below.at[part], bot_s.at[k], bot_r.at[k], down))

    for copy in z_out:
        copy.wait()
    total = z_in[0]
    for i in range(1, NZ):
        total = total + z_in[i]
    mine = 32 * core + 4 * y + x
    bar = total[16:24] + 1.0
    step = jnp.concatenate([total[0:8] / bar, total[8:16] / bar], 0)
    tiles[mine] = probe_tiles[mine] + step

    xg_out = []
    for i in far_first(NX):
        xg_out.append(send(tiles.at[mine], tiles.at[mine], xg_s.at[i], xg_r.at[i], place.along_x(i)))
    for copy in xg_out:
        copy.wait()
    block = pl.ds(32 * core + 4 * y, 4)
    yg_out = {}
    for i in far_first(NY):
        yg_out[i] = send(tiles.at[block], tiles.at[block], yg_s.at[i], yg_r.at[i], place.along_y(i))
    cg_out = [send(tiles.at[block], tiles.at[block], cg_s.at[0], cg_r.at[0], partner)]
    order = sorted(yg_out, key=lambda i: min(i, NY - i))
    for i in order:
        yg_out[i].wait_recv()
        came = lax.rem(y + NY - i, NY)
        part = pl.ds(32 * core + 4 * came, 4)
        cg_out.append(send(tiles.at[part], tiles.at[part], cg_s.at[i], cg_r.at[i], partner))

    side_out[CHUNKS].wait()
    new_obj[...] = obj[...] + (main[:, pl.ds(0, F), :] + jnp.where(first_col, 0.0, side[:, pl.ds(0, F), :]))
    for copy in bottom_out:
        copy.wait()
    first_row = place.row == 0
    new_obj[:, pl.ds(0, HALO), :] += jnp.where(first_row, 0.0, below[...])

    for i in order:
        yg_out[i].wait_send()
    for copy in cg_out:
        copy.wait()
    for t in range(32):
        for h in range(2):
            for c in range(2):
                new_probe[c, 8 * t : 8 * t + 8, HALF * h : HALF * h + HALF] = tiles[
                    2 * t + h, 8 * c : 8 * c + 8
                ]


def reduce_step(grad, sums, probe_tiles, obj):
    out = jax.ShapeDtypeStruct((2, F, F), F32)

    def vmem(*shape):
        return pltpu.VMEM(shape, F32)

    return pl.pallas_call(
        reduce_kernel,
        name="reduce",
        out_shape=(out, out),
        in_specs=[ANY_SPEC, VMEM_SPEC, VMEM_SPEC, VMEM_SPEC],
        out_specs=(VMEM_SPEC, VMEM_SPEC),
        scratch_shapes=[
            vmem(2, EXT, F),
            vmem(2, EXT, F),
            vmem(2, HALO, F),
            vmem(2, HALO, F),
            vmem(32, 24, HALF),
            vmem(32, 24, HALF),
            vmem(NY - 1, 4, 24, HALF),
            vmem(4, 24, HALF),
            vmem(NX - 1, 24, HALF),
            vmem(24, HALF),
            vmem(NZ, 24, HALF),
            vmem(64, 16, HALF),
            DMA,
            DMA,
            DMA,
            *[DMA((n,)) for n in (NY, NY, NX, NX, NZ, NZ, NX, NX, NY, NY, NY, NY)],
            DMA((CHUNKS + 1,)),
            DMA((CHUNKS + 1,)),
            DMA((CHUNKS,)),
            DMA((CHUNKS,)),
        ],
        compiler_params=pltpu.CompilerParams(collective_id=1, has_side_effects=True),
    )(grad, sums, probe_tiles, obj)


def body(object_field, probe_field, measured, positions):
    right, below, corner = halo_exchange(object_field)
    pos = positions.reshape(measured.shape[0], 2)
    grad, sums, probe_tiles = frame_step(
        pos, object_field, right, below, corner, probe_field, measured
    )
    return reduce_step(grad, sums, probe_tiles, object_field)


def solution(mesh):
    in_specs = (P(None, "row", "col"), P(), P("row", "col", None), P("row", "col"))
    out_specs = (P(None, "row", "col"), P())
    return jax.shard_map(body, mesh=mesh, in_specs=in_specs, out_specs=out_specs, check_vma=False)
```

```python
import functools
import math

import jax
import jax.numpy as jnp
import numpy as np
from jax import lax
from jax.experimental import pallas as pl
from jax.experimental.pallas import tpu as pltpu
from jax.sharding import PartitionSpec as P

MESH = pl.DeviceIdType.MESH
DMA = pltpu.SemaphoreType.DMA
F = 256
HALF = 128
HALO = 160
EXT = F + HALO
CHUNKS = 5
TALL = F + 8
WIDE = F + 128
DEEP = EXT + 8
STEP = HALO // CHUNKS
NX, NY, NZ = 4, 8, 12
COMPONENTS = (2, 0, 1)
F32 = jnp.float32
BF16 = jnp.bfloat16
VMEM_SPEC = pl.BlockSpec(memory_space=pltpu.VMEM)
ANY_SPEC = pl.BlockSpec(memory_space=pl.ANY)


class Place:
    def __init__(self):
        self.row = lax.axis_index("row")
        self.col = lax.axis_index("col")
        self.rows = lax.axis_size("row")
        self.cols = lax.axis_size("col")
        self.z = lax.div(self.row, 2)
        self.x = 2 * lax.rem(self.row, 2) + lax.div(self.col, 16)
        self.y = lax.rem(lax.div(self.col, 2), NY)
        self.core = lax.rem(self.col, 2)

    def at(self, x, y, z, core):
        return (2 * z + lax.div(x, 2), 16 * lax.rem(x, 2) + 2 * y + core)

    def partner(self):
        return self.at(self.x, self.y, self.z, 1 - self.core)

    def along_x(self, i):
        return self.at(lax.rem(self.x + i, NX), self.y, self.z, self.core)

    def along_y(self, i):
        return self.at(self.x, lax.rem(self.y + i, NY), self.z, self.core)

    def along_z(self, i):
        return self.at(self.x, self.y, lax.rem(self.z + i, NZ), self.core)

    def up(self):
        return (lax.rem(self.row + self.rows - 1, self.rows), self.col)

    def down(self):
        return (lax.rem(self.row + 1, self.rows), self.col)

    def left(self):
        return (self.row, lax.rem(self.col + self.cols - 1, self.cols))

    def right(self):
        return (self.row, lax.rem(self.col + 1, self.cols))


def meet(devices):
    barrier = pltpu.get_barrier_semaphore()
    for device in devices:
        pl.semaphore_signal(barrier, inc=1, device_id=device, device_id_type=MESH)
    pl.semaphore_wait(barrier, len(devices))


def send(src, dst, send_sem, recv_sem, device):
    copy = pltpu.make_async_remote_copy(
        src_ref=src,
        dst_ref=dst,
        send_sem=send_sem,
        recv_sem=recv_sem,
        device_id=device,
        device_id_type=MESH,
    )
    copy.start()
    return copy


def far_first(count):
    order = []
    for d in range(count // 2, 0, -1):
        order.append(d)
        if count - d != d:
            order.append(count - d)
    return order


def halo_kernel(
    obj, probe, measured, mats, twiddle, ext, ampl, probe_out, mats_out, twiddle_out,
    raw, row_s, row_r, col_s, col_r, cor_s, cor_r, own_s,
):
    place = Place()
    up, left = place.up(), place.left()
    loads = [
        pltpu.make_async_copy(src, dst, own_s.at[i])
        for i, (src, dst) in enumerate(
            (
                (measured, raw),
                (mats, mats_out),
                (obj, ext.at[:, pl.ds(0, F), pl.ds(0, F)]),
                (probe, probe_out),
                (twiddle, twiddle_out),
            )
        )
    ]
    for load in loads:
        load.start()
    meet((up, place.down(), left, place.right()))
    rows = []
    for k in range(CHUNKS):
        here, there = pl.ds(k * STEP, STEP), pl.ds(F + k * STEP, STEP)
        dst = ext.at[:, there, pl.ds(0, F)]
        rows.append(send(obj.at[:, here], dst, row_s.at[k], row_r.at[k], up))
    side = send(obj, ext.at[:, pl.ds(0, F), pl.ds(F, F)], col_s, col_r, left)

    loads[0].wait()
    loads[1].wait()
    across, down = mats_out[4], mats_out[5]

    def reorder(f, carry):
        parts = [dot(down, part).astype(BF16) for part in split(raw[f])]
        ampl[f] = dot(parts[0], across) + dot(parts[1], across)
        return carry

    lax.fori_loop(0, raw.shape[0], reorder, 0)

    corners = []
    for k in range(CHUNKS):
        there = pl.ds(F + k * STEP, STEP)
        src, dst = ext.at[:, there, pl.ds(0, F)], ext.at[:, there, pl.ds(F, F)]
        rows[k].wait_recv()
        corners.append(send(src, dst, cor_s.at[k], cor_r.at[k], left))
    for load in loads[2:]:
        load.wait()
    side.wait()
    for k in range(CHUNKS):
        rows[k].wait_send()
        corners[k].wait()

    @pl.when(place.col == place.cols - 1)
    def _():
        ext[:, :, F:] = jnp.zeros((2, DEEP, F), F32)

    @pl.when(place.row == place.rows - 1)
    def _():
        ext[:, F:, :] = jnp.zeros((2, DEEP - F, 2 * F), F32)


def in_hbm(array):
    return pltpu.with_memory_space_constraint(array, pltpu.HBM)


def halo_exchange(obj, probe, measured):
    mats, twiddle = tables()
    like = jax.ShapeDtypeStruct
    frames = measured.shape[0]
    return pl.pallas_call(
        halo_kernel,
        name="halo",
        out_shape=(
            like((2, DEEP, 2 * F), F32),
            like((frames, F, F), F32),
            like((2, F, F), F32),
            like(mats.shape, BF16),
            like(twiddle.shape, F32),
        ),
        in_specs=[pl.BlockSpec(memory_space=pltpu.HBM)] * 5,
        out_specs=(VMEM_SPEC,) * 5,
        scratch_shapes=[
            pltpu.VMEM((frames, F, F), F32),
            DMA((CHUNKS,)),
            DMA((CHUNKS,)),
            DMA,
            DMA,
            DMA((CHUNKS,)),
            DMA((CHUNKS,)),
            DMA((5,)),
        ],
        compiler_params=pltpu.CompilerParams(
            collective_id=0, has_side_effects=True, vmem_limit_bytes=12 << 20
        ),
    )(*(in_hbm(a) for a in (obj, probe, measured, jnp.asarray(mats), jnp.asarray(twiddle))))


def split(x):
    high = x.astype(BF16)
    return high, (x - high.astype(F32)).astype(BF16)


def dot(a, b):
    return jnp.dot(a, b, preferred_element_type=F32)


def left_mult(high, low, x):
    x_high, x_low = split(x)
    return dot(high, x_high) + (dot(high, x_low) + dot(low, x_high))


def right_mult(x, high, low):
    x_high, x_low = split(x)
    return dot(x_high, high) + (dot(x_low, high) + dot(x_high, low))


def tables():
    k = np.arange(HALF)
    angle = 2.0 * math.pi / HALF * (np.outer(k, k) % HALF)
    cos, sin = np.cos(angle) / 16.0, np.sin(angle) / 16.0
    t1 = np.block([[cos, sin], [-sin, cos]]).astype(np.float32)
    stack = []
    for t in (t1, t1.T):
        high = t.astype(jnp.bfloat16)
        stack += [high, (t - high.astype(np.float32)).astype(jnp.bfloat16)]
    order = np.zeros((F, F), np.float32)
    for v in range(HALF):
        order[2 * v, v] = 1.0
        order[2 * v + 1, HALF + v] = 1.0
    stack += [order.astype(jnp.bfloat16), order.T.astype(jnp.bfloat16)]
    turn = 2.0 * math.pi / F * k
    down = [np.broadcast_to(f(turn)[:, None], (HALF, HALF)) for f in (np.cos, np.sin)]
    across = [np.broadcast_to(f(turn)[None, :], (8, HALF)) for f in (np.cos, np.sin)]
    twiddle = np.concatenate(down + across, 0).astype(np.float32)
    return np.stack(stack), twiddle


def frame_kernel(
    pos, ext, ampl, probe, mats, twiddle, grad, sums, probe_tiles, acc, scale
):
    frame = pl.program_id(0)

    @pl.when(frame == 0)
    def _():
        grad[...] = jnp.zeros_like(grad)
        acc[...] = jnp.zeros_like(acc)
        p_re, p_im = probe[0], probe[1]
        power = jnp.max(p_re * p_re + p_im * p_im, axis=0, keepdims=True)
        top = jnp.max(power, axis=1, keepdims=True)
        scale[...] = 1.0 / jnp.broadcast_to(top, scale.shape)
        for t in range(32):
            for h in range(2):
                for c in range(2):
                    probe_tiles[2 * t + h, 8 * c : 8 * c + 8] = probe[
                        c, 8 * t : 8 * t + 8, HALF * h : HALF * h + HALF
                    ]

    dy, dx = pos[0, frame], pos[1, frame]
    r_dy, r_dx = lax.rem(dy, 8), lax.rem(dx, HALF)
    rows = pl.ds(pl.multiple_of(dy - r_dy, 8), TALL)
    lanes = pl.ds(pl.multiple_of(dx - r_dx, HALF), WIDE)
    back_dy, back_dx = lax.rem(TALL - r_dy, TALL), lax.rem(WIDE - r_dx, WIDE)

    def window(c):
        return pltpu.roll(pltpu.roll(ext[c, rows, lanes], back_dx, 1)[:, :F], back_dy, 0)[:F]

    o_re, o_im = window(0), window(1)
    p_re, p_im = probe[0], probe[1]
    t1_high, t1_low, t2_high, t2_low = (mats[i] for i in range(4))
    down_c = jnp.concatenate([twiddle[:HALF]] * 2, 1)
    down_s = jnp.concatenate([twiddle[HALF:F]] * 2, 1)
    over_c, over_s = twiddle[F : F + 1], twiddle[F + 8 : F + 9]

    w_re = p_re * o_re - p_im * o_im
    w_im = p_re * o_im + p_im * o_re
    d_re, d_im = w_re[:HALF] - w_re[HALF:], w_im[:HALF] - w_im[HALF:]
    a = jnp.concatenate([w_re[:HALF] + w_re[HALF:], w_im[:HALF] + w_im[HALF:]], 0)
    b = jnp.concatenate([d_re * down_c + d_im * down_s, d_im * down_c - d_re * down_s], 0)
    y_even, y_odd = left_mult(t1_high, t1_low, a), left_mult(t1_high, t1_low, b)
    x_re = jnp.concatenate([y_even[:HALF], y_odd[:HALF]], 0)
    x_im = jnp.concatenate([y_even[HALF:], y_odd[HALF:]], 0)
    d_re, d_im = x_re[:, :HALF] - x_re[:, HALF:], x_im[:, :HALF] - x_im[:, HALF:]
    a = jnp.concatenate([x_re[:, :HALF] + x_re[:, HALF:], x_im[:, :HALF] + x_im[:, HALF:]], 1)
    b = jnp.concatenate([d_re * over_c + d_im * over_s, d_im * over_c - d_re * over_s], 1)

    def fit(x, target):
        re, im = x[:, :HALF], x[:, HALF:]
        factor = target * jnp.minimum(lax.rsqrt(re * re + im * im), 2.0) - 1.0
        return jnp.concatenate([re * factor, im * factor], 1)

    s_even = fit(right_mult(a, t2_high, t2_low), ampl[0, :, :HALF])
    s_odd = fit(right_mult(b, t2_high, t2_low), ampl[0, :, HALF:])
    e, o = right_mult(s_even, t1_high, t1_low), right_mult(s_odd, t1_high, t1_low)
    e_re, e_im, o_re2, o_im2 = e[:, :HALF], e[:, HALF:], o[:, :HALF], o[:, HALF:]
    q_re, q_im = o_re2 * over_c - o_im2 * over_s, o_im2 * over_c + o_re2 * over_s
    x_re = jnp.concatenate([e_re + q_re, e_re - q_re], 1)
    x_im = jnp.concatenate([e_im + q_im, e_im - q_im], 1)
    e = left_mult(t2_high, t2_low, jnp.concatenate([x_re[:HALF], x_im[:HALF]], 0))
    o = left_mult(t2_high, t2_low, jnp.concatenate([x_re[HALF:], x_im[HALF:]], 0))
    e_re, e_im, o_re2, o_im2 = e[:HALF], e[HALF:], o[:HALF], o[HALF:]
    q_re, q_im = o_re2 * down_c - o_im2 * down_s, o_im2 * down_c + o_re2 * down_s
    c_re = jnp.concatenate([e_re + q_re, e_re - q_re], 0)
    c_im = jnp.concatenate([e_im + q_im, e_im - q_im], 0)

    acc[0] += o_re * c_re + o_im * c_im
    acc[1] += o_re * c_im - o_im * c_re
    acc[2] += o_re * o_re + o_im * o_im
    inverse = scale[0:1, 0:1]
    blank_rows, blank_lanes = jnp.zeros((TALL - F, F), F32), jnp.zeros((TALL, WIDE - F), F32)
    for c, g in ((0, p_re * c_re + p_im * c_im), (1, p_re * c_im - p_im * c_re)):
        moved = pltpu.roll(jnp.concatenate([g * inverse, blank_rows], 0), r_dy, 0)
        moved = pltpu.roll(jnp.concatenate([moved, blank_lanes], 1), r_dx, 1)
        grad[c, rows, lanes] += moved

    @pl.when(frame == pl.num_programs(0) - 1)
    def _():
        for t in range(32):
            for h in range(2):
                for c in range(3):
                    sums[c, 2 * t + h] = acc[
                        c, 8 * t : 8 * t + 8, HALF * h : HALF * h + HALF
                    ]


def frame_step(positions, ext, ampl, probe, mats, twiddle):
    def whole(shape):
        return pl.BlockSpec(shape, lambda f: (0,) * len(shape))

    return pl.pallas_call(
        frame_kernel,
        name="frames",
        grid=(ampl.shape[0],),
        out_shape=(
            jax.ShapeDtypeStruct((2, DEEP, 2 * F), F32),
            jax.ShapeDtypeStruct((3, 64, 8, HALF), F32),
            jax.ShapeDtypeStruct((64, 16, HALF), F32),
        ),
        in_specs=[
            pl.BlockSpec(memory_space=pltpu.SMEM),
            whole((2, DEEP, 2 * F)),
            pl.BlockSpec((1, F, F), lambda f: (f, 0, 0)),
            whole((2, F, F)),
            whole(mats.shape),
            whole(twiddle.shape),
        ],
        out_specs=(whole((2, DEEP, 2 * F)), whole((3, 64, 8, HALF)), whole((64, 16, HALF))),
        scratch_shapes=[pltpu.VMEM((3, F, F), F32), pltpu.VMEM((8, HALF), F32)],
        compiler_params=pltpu.CompilerParams(vmem_limit_bytes=28 << 20),
    )(positions, ext, ampl, probe, mats, twiddle)


def reduce_kernel(
    grad, sums, probe_tiles, grad_sum, tiles,
    main, side, below, bottom, core_in, half, x_in, x_sum, y_in, y_sum, z_in,
    local_s, core_s, core_r, x_s, x_r, y_s, y_r, z_s, z_r, yg_s, yg_r, xg_s, xg_r, cg_s, cg_r,
    side_s, side_r, bot_s, bot_r,
):
    place = Place()
    core, x, y, z = place.core, place.x, place.y, place.z
    partner, right, down = place.partner(), place.right(), place.down()
    peers = [partner, right, place.left(), down, place.up()]
    peers += [place.along_x(i) for i in range(1, NX)]
    peers += [place.along_y(i) for i in range(1, NY)]
    peers += [place.along_z(i) for i in range(1, NZ)]
    meet(peers)

    first = [
        send(sums.at[q, pl.ds(32 * (1 - core), 32)], core_in.at[q], core_s.at[q], core_r.at[q], partner)
        for q in COMPONENTS
    ]
    side_out = []

    def send_side(k):
        part = (slice(None), pl.ds(F + k * STEP, STEP) if k < CHUNKS else pl.ds(0, F))
        src = grad.at[part + (pl.ds(F, F),)]
        side_out.append(send(src, side.at[part], side_s.at[k], side_r.at[k], right))

    for k in range(CHUNKS):
        send_side(k)
    fetch = pltpu.make_async_copy(grad.at[:, pl.ds(0, EXT), pl.ds(0, F)], main, local_s)
    fetch.start()

    x_out, y_out, z_out = [], [], []
    for q, copy in zip(COMPONENTS, first):
        copy.wait_recv()
        half[q] = sums[q, pl.ds(32 * core, 32)] + core_in[q]
        out = []
        for i in far_first(NX):
            there = lax.rem(x + i, NX)
            part = half.at[q, pl.ds(NY * there, NY)]
            out.append(send(part, x_in.at[q, i - 1], x_s.at[q, i], x_r.at[q, i], place.along_x(i)))
        x_out.append(out)
    for q, copies in zip(COMPONENTS, x_out):
        for copy in copies:
            copy.wait_recv()
        total = half[q, pl.ds(NY * x, NY)]
        for i in range(NX - 1):
            total = total + x_in[q, i]
        x_sum[q] = total
        out = []
        for i in far_first(NY):
            there = lax.rem(y + i, NY)
            part = x_sum.at[q, there]
            out.append(send(part, y_in.at[q, i - 1], y_s.at[q, i], y_r.at[q, i], place.along_y(i)))
        y_out.append(out)
    send_side(CHUNKS)

    fetch.wait()
    first_col = place.col == 0
    bottom_out = []
    for k in range(CHUNKS):
        side_out[k].wait()
        rows = pl.ds(F + k * STEP, STEP)
        extra = jnp.where(first_col, 0.0, side[:, rows, :])
        bottom[:, pl.ds(k * STEP, STEP), :] = main[:, rows, :] + extra
        part = (slice(None), pl.ds(k * STEP, STEP))
        bottom_out.append(send(bottom.at[part], below.at[part], bot_s.at[k], bot_r.at[k], down))

    for q, copies in zip(COMPONENTS, y_out):
        for copy in copies:
            copy.wait_recv()
        total = x_sum[q, y]
        for i in range(NY - 1):
            total = total + y_in[q, i]
        y_sum[q] = total
        z_in[q, z] = total
        out = []
        for i in far_first(NZ):
            out.append(send(y_sum.at[q], z_in.at[q, z], z_s.at[q, i], z_r.at[q, i], place.along_z(i)))
        z_out.append(out)
    done = {}
    for q, copies in zip(COMPONENTS, z_out):
        for copy in copies:
            copy.wait_recv()
        total = z_in[q, 0]
        for i in range(1, NZ):
            total = total + z_in[q, i]
        done[q] = total
    base = 32 * core
    mine = base + NY * x + y
    bar = done[2] + 1.0
    tiles[mine] = probe_tiles[mine] + jnp.concatenate([done[0] / bar, done[1] / bar], 0)

    last = []

    def spread(tile, i):
        out = []
        for j in far_first(NX):
            out.append(send(tiles.at[tile], tiles.at[tile], xg_s.at[i, j], xg_r.at[i, j], place.along_x(j)))
        last.append(send(tiles.at[tile], tiles.at[tile], cg_s.at[i, 0], cg_r.at[i, 0], partner))
        return out

    yg_out, xg_out = {}, {}
    for i in far_first(NY):
        yg_out[i] = send(tiles.at[mine], tiles.at[mine], yg_s.at[i], yg_r.at[i], place.along_y(i))
    xg_out[0] = spread(mine, 0)
    order = sorted(yg_out, key=lambda i: min(i, NY - i))
    for i in order:
        yg_out[i].wait_recv()
        xg_out[i] = spread(base + NY * x + lax.rem(y + NY - i, NY), i)
    for i in [0] + order:
        for j, copy in zip(far_first(NX), xg_out[i]):
            copy.wait_recv()
            tile = base + NY * lax.rem(x + NX - j, NX) + lax.rem(y + NY - i, NY)
            last.append(send(tiles.at[tile], tiles.at[tile], cg_s.at[i, j], cg_r.at[i, j], partner))

    side_out[CHUNKS].wait()
    grad_sum[...] = main[:, pl.ds(0, F), :] + jnp.where(first_col, 0.0, side[:, pl.ds(0, F), :])
    for copy in bottom_out:
        copy.wait()
    first_row = place.row == 0
    grad_sum[:, pl.ds(0, HALO), :] += jnp.where(first_row, 0.0, below[...])
    for copies in [first, *x_out, *y_out, *z_out, yg_out.values(), *xg_out.values()]:
        for copy in copies:
            copy.wait_send()
    for copy in last:
        copy.wait()


def reduce_step(grad, sums, probe_tiles):
    def vmem(*shape):
        return pltpu.VMEM(shape, F32)

    return pl.pallas_call(
        reduce_kernel,
        name="reduce",
        out_shape=(
            jax.ShapeDtypeStruct((2, F, F), F32),
            jax.ShapeDtypeStruct((64, 16, HALF), F32),
        ),
        in_specs=[ANY_SPEC, VMEM_SPEC, VMEM_SPEC],
        out_specs=(VMEM_SPEC, VMEM_SPEC),
        scratch_shapes=[
            vmem(2, EXT, F),
            vmem(2, EXT, F),
            vmem(2, HALO, F),
            vmem(2, HALO, F),
            vmem(3, 32, 8, HALF),
            vmem(3, 32, 8, HALF),
            vmem(3, NX - 1, NY, 8, HALF),
            vmem(3, NY, 8, HALF),
            vmem(3, NY - 1, 8, HALF),
            vmem(3, 8, HALF),
            vmem(3, NZ, 8, HALF),
            DMA,
            *[DMA((3,))] * 2,
            *[DMA((3, NX))] * 2,
            *[DMA((3, NY))] * 2,
            *[DMA((3, NZ))] * 2,
            *[DMA((NY,))] * 2,
            *[DMA((NY, NX))] * 4,
            *[DMA((CHUNKS + 1,))] * 2,
            *[DMA((CHUNKS,))] * 2,
        ],
        compiler_params=pltpu.CompilerParams(
            collective_id=1, has_side_effects=True, vmem_limit_bytes=16 << 20
        ),
    )(grad, sums, probe_tiles)


def finish_kernel(obj, grad_sum, tiles, new_obj, new_probe):
    new_obj[...] = obj[...] + grad_sum[...]
    for t in range(32):
        for h in range(2):
            for c in range(2):
                new_probe[c, 8 * t : 8 * t + 8, HALF * h : HALF * h + HALF] = tiles[
                    2 * t + h, 8 * c : 8 * c + 8
                ]


def finish(obj, grad_sum, tiles):
    out = jax.ShapeDtypeStruct((2, F, F), F32)
    return pl.pallas_call(
        finish_kernel,
        name="finish",
        out_shape=(out, out),
        in_specs=[VMEM_SPEC] * 3,
        out_specs=(VMEM_SPEC, VMEM_SPEC),
        compiler_params=pltpu.CompilerParams(vmem_limit_bytes=12 << 20),
    )(obj, grad_sum, tiles)


def body(object_field, probe_field, measured, positions):
    shared = halo_exchange(object_field, probe_field, measured)
    grad, sums, probe_tiles = frame_step(positions.T, *shared)
    return finish(object_field, *reduce_step(grad, sums, probe_tiles))


def solution(mesh):
    in_specs = (P(None, "row", "col"), P(), P("row", "col", None), P("row", "col"))
    out_specs = (P(None, "row", "col"), P())
    return jax.shard_map(body, mesh=mesh, in_specs=in_specs, out_specs=out_specs, check_vma=False)
```

```python
import functools
import math

import jax
import jax.numpy as jnp
import numpy as np
from jax import lax
from jax.experimental import pallas as pl
from jax.experimental.pallas import tpu as pltpu
from jax.sharding import PartitionSpec as P

MESH = pl.DeviceIdType.MESH
DMA = pltpu.SemaphoreType.DMA
F = 256
HALF = 128
HALO = 160
EXT = F + HALO
CHUNKS = 5
TALL = F + 8
WIDE = F + 128
DEEP = EXT + 8
STEP = HALO // CHUNKS
NX, NY, NZ = 4, 8, 12
NEAR = 4
FAR = NZ // NEAR
COMPONENTS = (2, 0, 1)
BUNDLES = (pl.ds(2, 1), pl.ds(0, 2))
GROUPS = ((0, (1, 7)), (3, (2, 6)), (5, (3, 5, 4)))
SLOT_OF = (0, 1, 3, 5, 7, 6, 4, 2)
F32 = jnp.float32
BF16 = jnp.bfloat16
VMEM_SPEC = pl.BlockSpec(memory_space=pltpu.VMEM)
ANY_SPEC = pl.BlockSpec(memory_space=pl.ANY)


class Place:
    def __init__(self):
        self.row = lax.axis_index("row")
        self.col = lax.axis_index("col")
        self.rows = lax.axis_size("row")
        self.cols = lax.axis_size("col")
        self.z = lax.div(self.row, 2)
        self.x = 2 * lax.rem(self.row, 2) + lax.div(self.col, 16)
        self.y = lax.rem(lax.div(self.col, 2), NY)
        self.core = lax.rem(self.col, 2)

    def at(self, x, y, z, core):
        return (2 * z + lax.div(x, 2), 16 * lax.rem(x, 2) + 2 * y + core)

    def partner(self):
        return self.at(self.x, self.y, self.z, 1 - self.core)

    def along_x(self, i):
        return self.at(lax.rem(self.x + i, NX), self.y, self.z, self.core)

    def along_y(self, i):
        return self.at(self.x, lax.rem(self.y + i, NY), self.z, self.core)

    def near_z(self, i):
        z = NEAR * lax.div(self.z, NEAR) + lax.rem(self.z + i, NEAR)
        return self.at(self.x, self.y, z, self.core)

    def far_z(self, i):
        return self.at(self.x, self.y, lax.rem(self.z + NEAR * i, NZ), self.core)

    def up(self):
        return (lax.rem(self.row + self.rows - 1, self.rows), self.col)

    def down(self):
        return (lax.rem(self.row + 1, self.rows), self.col)

    def left(self):
        return (self.row, lax.rem(self.col + self.cols - 1, self.cols))

    def right(self):
        return (self.row, lax.rem(self.col + 1, self.cols))


def meet(devices):
    barrier = pltpu.get_barrier_semaphore()
    for device in devices:
        pl.semaphore_signal(barrier, inc=1, device_id=device, device_id_type=MESH)
    pl.semaphore_wait(barrier, len(devices))


def send(src, dst, send_sem, recv_sem, device):
    copy = pltpu.make_async_remote_copy(
        src_ref=src,
        dst_ref=dst,
        send_sem=send_sem,
        recv_sem=recv_sem,
        device_id=device,
        device_id_type=MESH,
    )
    copy.start()
    return copy


def far_first(count):
    order = []
    for d in range(count // 2, 0, -1):
        order.append(d)
        if count - d != d:
            order.append(count - d)
    return order


def halo_kernel(
    obj, probe, measured, mats, twiddle, ext, ampl, probe_out, mats_out, twiddle_out,
    raw, row_s, row_r, col_s, col_r, cor_s, cor_r, own_s,
):
    place = Place()
    up, left = place.up(), place.left()
    loads = [
        pltpu.make_async_copy(src, dst, own_s.at[i])
        for i, (src, dst) in enumerate(
            (
                (measured, raw),
                (mats, mats_out),
                (obj, ext.at[:, pl.ds(0, F), pl.ds(0, F)]),
                (probe, probe_out),
                (twiddle, twiddle_out),
            )
        )
    ]
    for load in loads:
        load.start()
    meet((up, place.down(), left, place.right()))
    rows = []
    for k in range(CHUNKS):
        here, there = pl.ds(k * STEP, STEP), pl.ds(F + k * STEP, STEP)
        dst = ext.at[:, there, pl.ds(0, F)]
        rows.append(send(obj.at[:, here], dst, row_s.at[k], row_r.at[k], up))
    side = send(obj, ext.at[:, pl.ds(0, F), pl.ds(F, F)], col_s, col_r, left)

    loads[0].wait()
    loads[1].wait()
    across, down = mats_out[4], mats_out[5]

    def reorder(f, carry):
        parts = [dot(down, part).astype(BF16) for part in split(raw[f])]
        ampl[f] = dot(parts[0], across) + dot(parts[1], across)
        return carry

    lax.fori_loop(0, raw.shape[0], reorder, 0)

    corners = []
    for k in range(CHUNKS):
        there = pl.ds(F + k * STEP, STEP)
        src, dst = ext.at[:, there, pl.ds(0, F)], ext.at[:, there, pl.ds(F, F)]
        rows[k].wait_recv()
        corners.append(send(src, dst, cor_s.at[k], cor_r.at[k], left))
    for load in loads[2:]:
        load.wait()
    side.wait()
    for k in range(CHUNKS):
        rows[k].wait_send()
        corners[k].wait()

    @pl.when(place.col == place.cols - 1)
    def _():
        ext[:, :, F:] = jnp.zeros((2, DEEP, F), F32)

    @pl.when(place.row == place.rows - 1)
    def _():
        ext[:, F:, :] = jnp.zeros((2, DEEP - F, 2 * F), F32)


def in_hbm(array):
    return pltpu.with_memory_space_constraint(array, pltpu.HBM)


def halo_exchange(obj, probe, measured):
    mats, twiddle = tables()
    like = jax.ShapeDtypeStruct
    frames = measured.shape[0]
    return pl.pallas_call(
        halo_kernel,
        name="halo",
        out_shape=(
            like((2, DEEP, 2 * F), F32),
            like((frames, F, F), F32),
            like((2, F, F), F32),
            like(mats.shape, BF16),
            like(twiddle.shape, F32),
        ),
        in_specs=[pl.BlockSpec(memory_space=pltpu.HBM)] * 5,
        out_specs=(VMEM_SPEC,) * 5,
        scratch_shapes=[
            pltpu.VMEM((frames, F, F), F32),
            DMA((CHUNKS,)),
            DMA((CHUNKS,)),
            DMA,
            DMA,
            DMA((CHUNKS,)),
            DMA((CHUNKS,)),
            DMA((5,)),
        ],
        compiler_params=pltpu.CompilerParams(
            collective_id=0, has_side_effects=True, vmem_limit_bytes=12 << 20
        ),
    )(*(in_hbm(a) for a in (obj, probe, measured, jnp.asarray(mats), jnp.asarray(twiddle))))


def split(x):
    high = x.astype(BF16)
    return high, (x - high.astype(F32)).astype(BF16)


def dot(a, b):
    return jnp.dot(a, b, preferred_element_type=F32)


def left_mult(high, low, x):
    x_high, x_low = split(x)
    return dot(high, x_high) + (dot(high, x_low) + dot(low, x_high))


def right_mult(x, high, low):
    x_high, x_low = split(x)
    return dot(x_high, high) + (dot(x_low, high) + dot(x_high, low))


def tables():
    k = np.arange(HALF)
    angle = 2.0 * math.pi / HALF * (np.outer(k, k) % HALF)
    cos, sin = np.cos(angle) / 16.0, np.sin(angle) / 16.0
    t1 = np.block([[cos, sin], [-sin, cos]]).astype(np.float32)
    stack = []
    for t in (t1, t1.T):
        high = t.astype(jnp.bfloat16)
        stack += [high, (t - high.astype(np.float32)).astype(jnp.bfloat16)]
    order = np.zeros((F, F), np.float32)
    for v in range(HALF):
        order[2 * v, v] = 1.0
        order[2 * v + 1, HALF + v] = 1.0
    stack += [order.astype(jnp.bfloat16), order.T.astype(jnp.bfloat16)]
    turn = 2.0 * math.pi / F * k
    down = [np.broadcast_to(f(turn)[:, None], (HALF, HALF)) for f in (np.cos, np.sin)]
    across = [np.broadcast_to(f(turn)[None, :], (8, HALF)) for f in (np.cos, np.sin)]
    twiddle = np.concatenate(down + across, 0).astype(np.float32)
    return np.stack(stack), twiddle


def frame_kernel(
    pos, ext, ampl, probe, mats, twiddle, grad, sums, probe_tiles, acc, scale
):
    step = pl.program_id(0)

    @pl.when(step == 0)
    def _():
        grad[...] = jnp.zeros_like(grad)
        acc[...] = jnp.zeros_like(acc)
        p_re, p_im = probe[0], probe[1]
        power = jnp.max(p_re * p_re + p_im * p_im, axis=0, keepdims=True)
        top = jnp.max(power, axis=1, keepdims=True)
        scale[...] = 1.0 / jnp.broadcast_to(top, scale.shape)
        for t in range(32):
            for h in range(2):
                for c in range(2):
                    probe_tiles[2 * t + h, 8 * c : 8 * c + 8] = probe[
                        c, 8 * t : 8 * t + 8, HALF * h : HALF * h + HALF
                    ]

    for k in range(2):
        dy, dx = pos[0, 2 * step + k], pos[1, 2 * step + k]
        r_dy, r_dx = lax.rem(dy, 8), lax.rem(dx, HALF)
        rows = pl.ds(pl.multiple_of(dy - r_dy, 8), TALL)
        lanes = pl.ds(pl.multiple_of(dx - r_dx, HALF), WIDE)
        back_dy, back_dx = lax.rem(TALL - r_dy, TALL), lax.rem(WIDE - r_dx, WIDE)

        def window(c):
            return pltpu.roll(pltpu.roll(ext[c, rows, lanes], back_dx, 1)[:, :F], back_dy, 0)[:F]

        o_re, o_im = window(0), window(1)
        p_re, p_im = probe[0], probe[1]
        t1_high, t1_low, t2_high, t2_low = (mats[i] for i in range(4))
        down_c = jnp.concatenate([twiddle[:HALF]] * 2, 1)
        down_s = jnp.concatenate([twiddle[HALF:F]] * 2, 1)
        over_c, over_s = twiddle[F : F + 1], twiddle[F + 8 : F + 9]

        w_re = p_re * o_re - p_im * o_im
        w_im = p_re * o_im + p_im * o_re
        d_re, d_im = w_re[:HALF] - w_re[HALF:], w_im[:HALF] - w_im[HALF:]
        a = jnp.concatenate([w_re[:HALF] + w_re[HALF:], w_im[:HALF] + w_im[HALF:]], 0)
        b = jnp.concatenate([d_re * down_c + d_im * down_s, d_im * down_c - d_re * down_s], 0)
        y_even, y_odd = left_mult(t1_high, t1_low, a), left_mult(t1_high, t1_low, b)
        x_re = jnp.concatenate([y_even[:HALF], y_odd[:HALF]], 0)
        x_im = jnp.concatenate([y_even[HALF:], y_odd[HALF:]], 0)
        d_re, d_im = x_re[:, :HALF] - x_re[:, HALF:], x_im[:, :HALF] - x_im[:, HALF:]
        a = jnp.concatenate([x_re[:, :HALF] + x_re[:, HALF:], x_im[:, :HALF] + x_im[:, HALF:]], 1)
        b = jnp.concatenate([d_re * over_c + d_im * over_s, d_im * over_c - d_re * over_s], 1)

        def fit(x, target):
            re, im = x[:, :HALF], x[:, HALF:]
            factor = target * jnp.minimum(lax.rsqrt(re * re + im * im), 2.0) - 1.0
            return jnp.concatenate([re * factor, im * factor], 1)

        s_even = fit(right_mult(a, t2_high, t2_low), ampl[k, :, :HALF])
        s_odd = fit(right_mult(b, t2_high, t2_low), ampl[k, :, HALF:])
        e, o = right_mult(s_even, t1_high, t1_low), right_mult(s_odd, t1_high, t1_low)
        e_re, e_im, o_re2, o_im2 = e[:, :HALF], e[:, HALF:], o[:, :HALF], o[:, HALF:]
        q_re, q_im = o_re2 * over_c - o_im2 * over_s, o_im2 * over_c + o_re2 * over_s
        x_re = jnp.concatenate([e_re + q_re, e_re - q_re], 1)
        x_im = jnp.concatenate([e_im + q_im, e_im - q_im], 1)
        e = left_mult(t2_high, t2_low, jnp.concatenate([x_re[:HALF], x_im[:HALF]], 0))
        o = left_mult(t2_high, t2_low, jnp.concatenate([x_re[HALF:], x_im[HALF:]], 0))
        e_re, e_im, o_re2, o_im2 = e[:HALF], e[HALF:], o[:HALF], o[HALF:]
        q_re, q_im = o_re2 * down_c - o_im2 * down_s, o_im2 * down_c + o_re2 * down_s
        c_re = jnp.concatenate([e_re + q_re, e_re - q_re], 0)
        c_im = jnp.concatenate([e_im + q_im, e_im - q_im], 0)

        acc[0] += o_re * c_re + o_im * c_im
        acc[1] += o_re * c_im - o_im * c_re
        acc[2] += o_re * o_re + o_im * o_im
        inverse = scale[0:1, 0:1]
        blank_rows, blank_lanes = jnp.zeros((TALL - F, F), F32), jnp.zeros((TALL, WIDE - F), F32)
        for c, g in ((0, p_re * c_re + p_im * c_im), (1, p_re * c_im - p_im * c_re)):
            moved = pltpu.roll(jnp.concatenate([g * inverse, blank_rows], 0), r_dy, 0)
            moved = pltpu.roll(jnp.concatenate([moved, blank_lanes], 1), r_dx, 1)
            grad[c, rows, lanes] += moved

    @pl.when(step == pl.num_programs(0) - 1)
    def _():
        for t in range(32):
            for h in range(2):
                for c in range(3):
                    sums[c, 2 * t + h] = acc[
                        c, 8 * t : 8 * t + 8, HALF * h : HALF * h + HALF
                    ]


def frame_step(positions, ext, ampl, probe, mats, twiddle):
    def whole(shape):
        return pl.BlockSpec(shape, lambda f: (0,) * len(shape))

    return pl.pallas_call(
        frame_kernel,
        name="frames",
        grid=(ampl.shape[0] // 2,),
        out_shape=(
            jax.ShapeDtypeStruct((2, DEEP, 2 * F), F32),
            jax.ShapeDtypeStruct((3, 64, 8, HALF), F32),
            jax.ShapeDtypeStruct((64, 16, HALF), F32),
        ),
        in_specs=[
            pl.BlockSpec(memory_space=pltpu.SMEM),
            whole((2, DEEP, 2 * F)),
            pl.BlockSpec((2, F, F), lambda f: (f, 0, 0)),
            whole((2, F, F)),
            whole(mats.shape),
            whole(twiddle.shape),
        ],
        out_specs=(whole((2, DEEP, 2 * F)), whole((3, 64, 8, HALF)), whole((64, 16, HALF))),
        scratch_shapes=[pltpu.VMEM((3, F, F), F32), pltpu.VMEM((8, HALF), F32)],
        compiler_params=pltpu.CompilerParams(vmem_limit_bytes=28 << 20),
    )(positions, ext, ampl, probe, mats, twiddle)


def reduce_kernel(
    grad, sums, probe_tiles, grad_sum, tiles,
    main, side, below, bottom, core_in, half, x_in, x_sum, y_in, y_sum, near_in, near_sum, far_in,
    local_s, core_s, core_r, x_s, x_r, y_s, y_r, n_s, n_r, f_s, f_r, yg_s, yg_r, xg_s, xg_r, cg_s, cg_r,
    side_s, side_r, bot_s, bot_r,
):
    place = Place()
    core, x, y, z = place.core, place.x, place.y, place.z
    partner, right, down = place.partner(), place.right(), place.down()
    peers = [partner, right, place.left(), down, place.up()]
    peers += [place.along_x(i) for i in range(1, NX)]
    peers += [place.along_y(i) for i in range(1, NY)]
    peers += [place.near_z(i) for i in range(1, NEAR)]
    peers += [place.far_z(i) for i in range(1, FAR)]
    meet(peers)

    first = [
        send(sums.at[q, pl.ds(32 * (1 - core), 32)], core_in.at[q], core_s.at[q], core_r.at[q], partner)
        for q in COMPONENTS
    ]
    side_out = []

    def send_side(k):
        part = (slice(None), pl.ds(F + k * STEP, STEP) if k < CHUNKS else pl.ds(0, F))
        src = grad.at[part + (pl.ds(F, F),)]
        side_out.append(send(src, side.at[part], side_s.at[k], side_r.at[k], right))

    for k in range(CHUNKS):
        send_side(k)
    fetch = pltpu.make_async_copy(grad.at[:, pl.ds(0, EXT), pl.ds(0, F)], main, local_s)
    fetch.start()

    x_out, y_out, near_out, far_out = [], [], [], []
    for q, copy in zip(COMPONENTS, first):
        copy.wait_recv()
        half[q] = sums[q, pl.ds(32 * core, 32)] + core_in[q]
        out = []
        for i in far_first(NX):
            there = lax.rem(x + i, NX)
            part = half.at[q, pl.ds(NY * there, NY)]
            out.append(send(part, x_in.at[q, i - 1], x_s.at[q, i], x_r.at[q, i], place.along_x(i)))
        x_out.append(out)
    waiting = dict(zip(COMPONENTS, x_out))
    for b, bundle in enumerate(BUNDLES):
        for q in ((2,), (0, 1))[b]:
            for copy in waiting[q]:
                copy.wait_recv()
            total = half[q, pl.ds(NY * x, NY)]
            for i in range(NX - 1):
                total = total + x_in[q, i]
            x_sum[q] = total
        out = []
        for i in far_first(NY):
            there = lax.rem(y + i, NY)
            part, dst = x_sum.at[bundle, there], y_in.at[bundle, i - 1]
            out.append(send(part, dst, y_s.at[b, i], y_r.at[b, i], place.along_y(i)))
        y_out.append(out)
    send_side(CHUNKS)

    fetch.wait()
    first_col = place.col == 0
    bottom_out = []
    for k in range(CHUNKS):
        side_out[k].wait()
        rows = pl.ds(F + k * STEP, STEP)
        extra = jnp.where(first_col, 0.0, side[:, rows, :])
        bottom[:, pl.ds(k * STEP, STEP), :] = main[:, rows, :] + extra
        part = (slice(None), pl.ds(k * STEP, STEP))
        bottom_out.append(send(bottom.at[part], below.at[part], bot_s.at[k], bot_r.at[k], down))

    in_near, in_far = lax.rem(z, NEAR), lax.div(z, NEAR)
    for b, bundle in enumerate(BUNDLES):
        for copy in y_out[b]:
            copy.wait_recv()
        total = x_sum[bundle, y]
        for i in range(NY - 1):
            total = total + y_in[bundle, i]
        y_sum[bundle] = total
        near_in[bundle, in_near] = total
        out = []
        for i in range(1, NEAR):
            dst = near_in.at[bundle, in_near]
            out.append(send(y_sum.at[bundle], dst, n_s.at[b, i], n_r.at[b, i], place.near_z(i)))
        near_out.append(out)
    for b, bundle in enumerate(BUNDLES):
        for copy in near_out[b]:
            copy.wait_recv()
        total = near_in[bundle, 0]
        for i in range(1, NEAR):
            total = total + near_in[bundle, i]
        near_sum[bundle] = total
        far_in[bundle, in_far] = total
        out = []
        for i in range(1, FAR):
            dst = far_in.at[bundle, in_far]
            out.append(send(near_sum.at[bundle], dst, f_s.at[b, i], f_r.at[b, i], place.far_z(i)))
        far_out.append(out)
    for copies in far_out:
        for copy in copies:
            copy.wait_recv()
    done = far_in[:, 0]
    for i in range(1, FAR):
        done = done + far_in[:, i]
    base = 32 * core
    mine = base + NY * x + y
    home = base + NY * x
    bar = done[2] + 1.0
    tiles[home] = probe_tiles[mine] + jnp.concatenate([done[0] / bar, done[1] / bar], 0)

    yg_out = {}
    for i in far_first(NY):
        dst = tiles.at[home + SLOT_OF[NY - i]]
        yg_out[i] = send(tiles.at[home], dst, yg_s.at[i], yg_r.at[i], place.along_y(i))
    last, xg_out = [], []
    ends = [start for start, _ in GROUPS[1:]] + [NY]
    for g, (start, offsets) in enumerate(GROUPS):
        for offset in offsets:
            yg_out[NY - offset].wait_recv()
        part = tiles.at[pl.ds(home + start, ends[g] - start)]
        out = []
        for j in far_first(NX):
            out.append(send(part, part, xg_s.at[g, j], xg_r.at[g, j], place.along_x(j)))
        xg_out.append(out)
        last.append(send(part, part, cg_s.at[g, 0], cg_r.at[g, 0], partner))
    for g, (start, _) in enumerate(GROUPS):
        for j, copy in zip(far_first(NX), xg_out[g]):
            copy.wait_recv()
            there = base + NY * lax.rem(x + NX - j, NX) + start
            part = tiles.at[pl.ds(there, ends[g] - start)]
            last.append(send(part, part, cg_s.at[g, j], cg_r.at[g, j], partner))

    side_out[CHUNKS].wait()
    grad_sum[...] = main[:, pl.ds(0, F), :] + jnp.where(first_col, 0.0, side[:, pl.ds(0, F), :])
    for copy in bottom_out:
        copy.wait()
    first_row = place.row == 0
    grad_sum[:, pl.ds(0, HALO), :] += jnp.where(first_row, 0.0, below[...])
    for copies in [first, *x_out, *y_out, *near_out, *far_out, yg_out.values(), *xg_out]:
        for copy in copies:
            copy.wait_send()
    for copy in last:
        copy.wait()


def reduce_step(grad, sums, probe_tiles):
    def vmem(*shape):
        return pltpu.VMEM(shape, F32)

    return pl.pallas_call(
        reduce_kernel,
        name="reduce",
        out_shape=(
            jax.ShapeDtypeStruct((2, F, F), F32),
            jax.ShapeDtypeStruct((64, 16, HALF), F32),
        ),
        in_specs=[ANY_SPEC, VMEM_SPEC, VMEM_SPEC],
        out_specs=(VMEM_SPEC, VMEM_SPEC),
        scratch_shapes=[
            vmem(2, EXT, F),
            vmem(2, EXT, F),
            vmem(2, HALO, F),
            vmem(2, HALO, F),
            vmem(3, 32, 8, HALF),
            vmem(3, 32, 8, HALF),
            vmem(3, NX - 1, NY, 8, HALF),
            vmem(3, NY, 8, HALF),
            vmem(3, NY - 1, 8, HALF),
            vmem(3, 8, HALF),
            vmem(3, NEAR, 8, HALF),
            vmem(3, 8, HALF),
            vmem(3, FAR, 8, HALF),
            DMA,
            *[DMA((3,))] * 2,
            *[DMA((3, NX))] * 2,
            *[DMA((2, NY))] * 2,
            *[DMA((2, NEAR))] * 2,
            *[DMA((2, FAR))] * 2,
            *[DMA((NY,))] * 2,
            *[DMA((len(GROUPS), NX))] * 4,
            *[DMA((CHUNKS + 1,))] * 2,
            *[DMA((CHUNKS,))] * 2,
        ],
        compiler_params=pltpu.CompilerParams(
            collective_id=1, has_side_effects=True, vmem_limit_bytes=16 << 20
        ),
    )(grad, sums, probe_tiles)


def finish_kernel(obj, grad_sum, tiles, new_obj, new_probe):
    new_obj[...] = obj[...] + grad_sum[...]
    y = Place().y
    for there in range(NY):
        off = lax.rem(there + NY - y, NY)
        late = jnp.where(off > 4, 2 * (NY - off), 2 * off - 1)
        slot = jnp.where(off == 0, 0, late)
        for block in range(8):
            t, h = divmod(NY * block + there, 2)
            tile = tiles[NY * block + slot]
            for c in range(2):
                new_probe[c, 8 * t : 8 * t + 8, HALF * h : HALF * h + HALF] = tile[8 * c : 8 * c + 8]


def finish(obj, grad_sum, tiles):
    out = jax.ShapeDtypeStruct((2, F, F), F32)
    return pl.pallas_call(
        finish_kernel,
        name="finish",
        out_shape=(out, out),
        in_specs=[VMEM_SPEC] * 3,
        out_specs=(VMEM_SPEC, VMEM_SPEC),
        compiler_params=pltpu.CompilerParams(vmem_limit_bytes=12 << 20),
    )(obj, grad_sum, tiles)


def body(object_field, probe_field, measured, positions):
    shared = halo_exchange(object_field, probe_field, measured)
    grad, sums, probe_tiles = frame_step(positions.T, *shared)
    return finish(object_field, *reduce_step(grad, sums, probe_tiles))


def solution(mesh):
    in_specs = (P(None, "row", "col"), P(), P("row", "col", None), P("row", "col"))
    out_specs = (P(None, "row", "col"), P())
    return jax.shard_map(body, mesh=mesh, in_specs=in_specs, out_specs=out_specs, check_vma=False)
```

```python
import functools
import math

import jax
import jax.numpy as jnp
import numpy as np
from jax import lax
from jax.experimental import pallas as pl
from jax.experimental.pallas import tpu as pltpu
from jax.sharding import PartitionSpec as P

MESH = pl.DeviceIdType.MESH
DMA = pltpu.SemaphoreType.DMA
F = 256
HALF = 128
HALO = 160
EXT = F + HALO
CHUNKS = 5
TALL = F + 8
WIDE = F + 128
DEEP = EXT + 8
STEP = HALO // CHUNKS
PARTS = 10
PART = HALO // PARTS
NX, NY, NZ = 4, 8, 12
NEAR = 4
FAR = NZ // NEAR
COMPONENTS = (2, 0, 1)
BUNDLES = (pl.ds(2, 1), pl.ds(0, 2))
GROUPS = ((0, (1, 7)), (3, (2, 6)), (5, (3, 5, 4)))
SLOT_OF = (0, 1, 3, 5, 7, 6, 4, 2)
F32 = jnp.float32
BF16 = jnp.bfloat16
VMEM_SPEC = pl.BlockSpec(memory_space=pltpu.VMEM)
ANY_SPEC = pl.BlockSpec(memory_space=pl.ANY)


class Place:
    def __init__(self):
        self.row = lax.axis_index("row")
        self.col = lax.axis_index("col")
        self.rows = lax.axis_size("row")
        self.cols = lax.axis_size("col")
        self.z = lax.div(self.row, 2)
        self.x = 2 * lax.rem(self.row, 2) + lax.div(self.col, 16)
        self.y = lax.rem(lax.div(self.col, 2), NY)
        self.core = lax.rem(self.col, 2)

    def at(self, x, y, z, core):
        return (2 * z + lax.div(x, 2), 16 * lax.rem(x, 2) + 2 * y + core)

    def partner(self):
        return self.at(self.x, self.y, self.z, 1 - self.core)

    def along_x(self, i):
        return self.at(lax.rem(self.x + i, NX), self.y, self.z, self.core)

    def along_y(self, i):
        return self.at(self.x, lax.rem(self.y + i, NY), self.z, self.core)

    def near_z(self, i):
        z = NEAR * lax.div(self.z, NEAR) + lax.rem(self.z + i, NEAR)
        return self.at(self.x, self.y, z, self.core)

    def far_z(self, i):
        return self.at(self.x, self.y, lax.rem(self.z + NEAR * i, NZ), self.core)

    def up(self):
        return (lax.rem(self.row + self.rows - 1, self.rows), self.col)

    def down(self):
        return (lax.rem(self.row + 1, self.rows), self.col)

    def left(self):
        return (self.row, lax.rem(self.col + self.cols - 1, self.cols))

    def right(self):
        return (self.row, lax.rem(self.col + 1, self.cols))


def meet(devices):
    barrier = pltpu.get_barrier_semaphore()
    for device in devices:
        pl.semaphore_signal(barrier, inc=1, device_id=device, device_id_type=MESH)
    pl.semaphore_wait(barrier, len(devices))


def send(src, dst, send_sem, recv_sem, device):
    copy = pltpu.make_async_remote_copy(
        src_ref=src,
        dst_ref=dst,
        send_sem=send_sem,
        recv_sem=recv_sem,
        device_id=device,
        device_id_type=MESH,
    )
    copy.start()
    return copy


def far_first(count):
    order = []
    for d in range(count // 2, 0, -1):
        order.append(d)
        if count - d != d:
            order.append(count - d)
    return order


def halo_kernel(
    obj, probe, measured, mats, twiddle, ext, ampl, probe_out, mats_out, twiddle_out,
    raw, row_s, row_r, col_s, col_r, cor_s, cor_r, own_s,
):
    place = Place()
    up, left = place.up(), place.left()
    loads = [
        pltpu.make_async_copy(src, dst, own_s.at[i])
        for i, (src, dst) in enumerate(
            (
                (measured, raw),
                (mats, mats_out),
                (obj, ext.at[:, pl.ds(0, F), pl.ds(0, F)]),
                (probe, probe_out),
                (twiddle, twiddle_out),
            )
        )
    ]
    barrier = pltpu.get_barrier_semaphore()
    peers = (up, place.down(), left, place.right())
    for device in peers:
        pl.semaphore_signal(barrier, inc=1, device_id=device, device_id_type=MESH)
    for load in loads:
        load.start()
    pl.semaphore_wait(barrier, len(peers))
    rows = []
    for k in range(PARTS):
        here, there = pl.ds(k * PART, PART), pl.ds(F + k * PART, PART)
        dst = ext.at[:, there, pl.ds(0, F)]
        rows.append(send(obj.at[:, here], dst, row_s.at[k], row_r.at[k], up))
    side = send(obj, ext.at[:, pl.ds(0, F), pl.ds(F, F)], col_s, col_r, left)

    loads[0].wait()
    loads[1].wait()
    across, down = mats_out[4], mats_out[5]

    def reorder(f, carry):
        parts = [dot(down, part).astype(BF16) for part in split(raw[f])]
        ampl[f] = dot(parts[0], across) + dot(parts[1], across)
        return carry

    lax.fori_loop(0, raw.shape[0], reorder, 0)

    corners = []
    for k in range(PARTS):
        there = pl.ds(F + k * PART, PART)
        src, dst = ext.at[:, there, pl.ds(0, F)], ext.at[:, there, pl.ds(F, F)]
        rows[k].wait_recv()
        corners.append(send(src, dst, cor_s.at[k], cor_r.at[k], left))
    for load in loads[2:]:
        load.wait()
    side.wait()
    for k in range(PARTS):
        rows[k].wait_send()
        corners[k].wait()

    @pl.when(place.col == place.cols - 1)
    def _():
        ext[:, :, F:] = jnp.zeros((2, DEEP, F), F32)

    @pl.when(place.row == place.rows - 1)
    def _():
        ext[:, F:, :] = jnp.zeros((2, DEEP - F, 2 * F), F32)


def in_hbm(array):
    return pltpu.with_memory_space_constraint(array, pltpu.HBM)


def halo_exchange(obj, probe, measured):
    mats, twiddle = tables()
    like = jax.ShapeDtypeStruct
    frames = measured.shape[0]
    return pl.pallas_call(
        halo_kernel,
        name="halo",
        out_shape=(
            like((2, DEEP, 2 * F), F32),
            like((frames, F, F), F32),
            like((2, F, F), F32),
            like(mats.shape, BF16),
            like(twiddle.shape, F32),
        ),
        in_specs=[pl.BlockSpec(memory_space=pltpu.HBM)] * 5,
        out_specs=(VMEM_SPEC,) * 5,
        scratch_shapes=[
            pltpu.VMEM((frames, F, F), F32),
            DMA((PARTS,)),
            DMA((PARTS,)),
            DMA,
            DMA,
            DMA((PARTS,)),
            DMA((PARTS,)),
            DMA((5,)),
        ],
        compiler_params=pltpu.CompilerParams(
            collective_id=0, has_side_effects=True, vmem_limit_bytes=12 << 20
        ),
    )(*(in_hbm(a) for a in (obj, probe, measured, jnp.asarray(mats), jnp.asarray(twiddle))))


def split(x):
    high = x.astype(BF16)
    return high, (x - high.astype(F32)).astype(BF16)


def dot(a, b):
    return jnp.dot(a, b, preferred_element_type=F32)


def left_mult(high, low, x):
    x_high, x_low = split(x)
    return dot(high, x_high) + (dot(high, x_low) + dot(low, x_high))


def right_mult(x, high, low):
    x_high, x_low = split(x)
    return dot(x_high, high) + (dot(x_low, high) + dot(x_high, low))


def tables():
    k = np.arange(HALF)
    angle = 2.0 * math.pi / HALF * (np.outer(k, k) % HALF)
    cos, sin = np.cos(angle) / 16.0, np.sin(angle) / 16.0
    t1 = np.block([[cos, sin], [-sin, cos]]).astype(np.float32)
    stack = []
    for t in (t1, t1.T):
        high = t.astype(jnp.bfloat16)
        stack += [high, (t - high.astype(np.float32)).astype(jnp.bfloat16)]
    order = np.zeros((F, F), np.float32)
    for v in range(HALF):
        order[2 * v, v] = 1.0
        order[2 * v + 1, HALF + v] = 1.0
    stack += [order.astype(jnp.bfloat16), order.T.astype(jnp.bfloat16)]
    turn = 2.0 * math.pi / F * k
    down = [np.broadcast_to(f(turn)[:, None], (HALF, HALF)) for f in (np.cos, np.sin)]
    across = [np.broadcast_to(f(turn)[None, :], (8, HALF)) for f in (np.cos, np.sin)]
    twiddle = np.concatenate(down + across, 0).astype(np.float32)
    return np.stack(stack), twiddle


def frame_kernel(
    pos, ext, ampl, probe, mats, twiddle, grad, sums, probe_tiles, acc, scale
):
    step = pl.program_id(0)

    @pl.when(step == 0)
    def _():
        grad[...] = jnp.zeros_like(grad)
        acc[...] = jnp.zeros_like(acc)
        p_re, p_im = probe[0], probe[1]
        power = jnp.max(p_re * p_re + p_im * p_im, axis=0, keepdims=True)
        top = jnp.max(power, axis=1, keepdims=True)
        scale[...] = 1.0 / jnp.broadcast_to(top, scale.shape)
        for t in range(32):
            for h in range(2):
                for c in range(2):
                    probe_tiles[2 * t + h, 8 * c : 8 * c + 8] = probe[
                        c, 8 * t : 8 * t + 8, HALF * h : HALF * h + HALF
                    ]

    for k in range(2):
        dy, dx = pos[0, 2 * step + k], pos[1, 2 * step + k]
        r_dy, r_dx = lax.rem(dy, 8), lax.rem(dx, HALF)
        rows = pl.ds(pl.multiple_of(dy - r_dy, 8), TALL)
        lanes = pl.ds(pl.multiple_of(dx - r_dx, HALF), WIDE)
        lane = lax.broadcasted_iota(jnp.int32, (TALL, HALF), 1)
        line = lax.broadcasted_iota(jnp.int32, (32, 8, F), 1)
        back_dy, back_dx = lax.rem(8 - r_dy, 8), lax.rem(HALF - r_dx, HALF)

        def window(c):
            wide = ext[c, rows, lanes]
            turned = [pltpu.roll(wide[:, HALF * j : HALF * j + HALF], back_dx, 1) for j in range(3)]
            keep = lane < HALF - r_dx
            tall = jnp.concatenate([jnp.where(keep, turned[j], turned[j + 1]) for j in range(2)], 1)
            tall = pltpu.roll(tall.reshape(33, 8, F), back_dy, 1)
            return jnp.where(line < 8 - r_dy, tall[:32], tall[1:]).reshape(F, F)

        o_re, o_im = window(0), window(1)
        p_re, p_im = probe[0], probe[1]
        t1_high, t1_low, t2_high, t2_low = (mats[i] for i in range(4))
        down_c = jnp.concatenate([twiddle[:HALF]] * 2, 1)
        down_s = jnp.concatenate([twiddle[HALF:F]] * 2, 1)
        over_c, over_s = twiddle[F : F + 1], twiddle[F + 8 : F + 9]

        w_re = p_re * o_re - p_im * o_im
        w_im = p_re * o_im + p_im * o_re
        d_re, d_im = w_re[:HALF] - w_re[HALF:], w_im[:HALF] - w_im[HALF:]
        a = jnp.concatenate([w_re[:HALF] + w_re[HALF:], w_im[:HALF] + w_im[HALF:]], 0)
        b = jnp.concatenate([d_re * down_c + d_im * down_s, d_im * down_c - d_re * down_s], 0)
        y_even, y_odd = left_mult(t1_high, t1_low, a), left_mult(t1_high, t1_low, b)
        x_re = jnp.concatenate([y_even[:HALF], y_odd[:HALF]], 0)
        x_im = jnp.concatenate([y_even[HALF:], y_odd[HALF:]], 0)
        d_re, d_im = x_re[:, :HALF] - x_re[:, HALF:], x_im[:, :HALF] - x_im[:, HALF:]
        a = jnp.concatenate([x_re[:, :HALF] + x_re[:, HALF:], x_im[:, :HALF] + x_im[:, HALF:]], 1)
        b = jnp.concatenate([d_re * over_c + d_im * over_s, d_im * over_c - d_re * over_s], 1)

        def fit(x, target):
            re, im = x[:, :HALF], x[:, HALF:]
            factor = target * jnp.minimum(lax.rsqrt(re * re + im * im), 2.0) - 1.0
            return jnp.concatenate([re * factor, im * factor], 1)

        s_even = fit(right_mult(a, t2_high, t2_low), ampl[k, :, :HALF])
        s_odd = fit(right_mult(b, t2_high, t2_low), ampl[k, :, HALF:])
        e, o = right_mult(s_even, t1_high, t1_low), right_mult(s_odd, t1_high, t1_low)
        e_re, e_im, o_re2, o_im2 = e[:, :HALF], e[:, HALF:], o[:, :HALF], o[:, HALF:]
        q_re, q_im = o_re2 * over_c - o_im2 * over_s, o_im2 * over_c + o_re2 * over_s
        x_re = jnp.concatenate([e_re + q_re, e_re - q_re], 1)
        x_im = jnp.concatenate([e_im + q_im, e_im - q_im], 1)
        e = left_mult(t2_high, t2_low, jnp.concatenate([x_re[:HALF], x_im[:HALF]], 0))
        o = left_mult(t2_high, t2_low, jnp.concatenate([x_re[HALF:], x_im[HALF:]], 0))
        e_re, e_im, o_re2, o_im2 = e[:HALF], e[HALF:], o[:HALF], o[HALF:]
        q_re, q_im = o_re2 * down_c - o_im2 * down_s, o_im2 * down_c + o_re2 * down_s
        c_re = jnp.concatenate([e_re + q_re, e_re - q_re], 0)
        c_im = jnp.concatenate([e_im + q_im, e_im - q_im], 0)

        acc[0] += o_re * c_re + o_im * c_im
        acc[1] += o_re * c_im - o_im * c_re
        acc[2] += o_re * o_re + o_im * o_im
        inverse = scale[0:1, 0:1]
        blank = jnp.zeros((1, 8, F), F32)
        edge = jnp.zeros((TALL, HALF), F32)
        below = lax.broadcasted_iota(jnp.int32, (33, 8, F), 1) >= r_dy
        beyond = lane >= r_dx
        for c, g in ((0, p_re * c_re + p_im * c_im), (1, p_re * c_im - p_im * c_re)):
            turned = pltpu.roll((g * inverse).reshape(32, 8, F), r_dy, 1)
            moved = jnp.where(
                below, jnp.concatenate([turned, blank], 0), jnp.concatenate([blank, turned], 0)
            ).reshape(TALL, F)
            first = pltpu.roll(moved[:, :HALF], r_dx, 1)
            second = pltpu.roll(moved[:, HALF:], r_dx, 1)
            grad[c, rows, lanes] += jnp.concatenate(
                [
                    jnp.where(beyond, first, edge),
                    jnp.where(beyond, second, first),
                    jnp.where(beyond, edge, second),
                ],
                1,
            )

    @pl.when(step == pl.num_programs(0) - 1)
    def _():
        for t in range(32):
            for h in range(2):
                for c in range(3):
                    sums[c, 2 * t + h] = acc[
                        c, 8 * t : 8 * t + 8, HALF * h : HALF * h + HALF
                    ]


def frame_step(positions, ext, ampl, probe, mats, twiddle):
    def whole(shape):
        return pl.BlockSpec(shape, lambda f: (0,) * len(shape))

    return pl.pallas_call(
        frame_kernel,
        name="frames",
        grid=(ampl.shape[0] // 2,),
        out_shape=(
            jax.ShapeDtypeStruct((2, DEEP, 2 * F), F32),
            jax.ShapeDtypeStruct((3, 64, 8, HALF), F32),
            jax.ShapeDtypeStruct((64, 16, HALF), F32),
        ),
        in_specs=[
            pl.BlockSpec(memory_space=pltpu.SMEM),
            whole((2, DEEP, 2 * F)),
            pl.BlockSpec((2, F, F), lambda f: (f, 0, 0)),
            whole((2, F, F)),
            whole(mats.shape),
            whole(twiddle.shape),
        ],
        out_specs=(whole((2, DEEP, 2 * F)), whole((3, 64, 8, HALF)), whole((64, 16, HALF))),
        scratch_shapes=[pltpu.VMEM((3, F, F), F32), pltpu.VMEM((8, HALF), F32)],
        compiler_params=pltpu.CompilerParams(vmem_limit_bytes=28 << 20),
    )(positions, ext, ampl, probe, mats, twiddle)


def reduce_kernel(
    grad, sums, probe_tiles, grad_sum, tiles,
    main, side, below, bottom, core_in, half, x_in, x_sum, y_in, y_sum, near_in, near_sum, far_in,
    local_s, core_s, core_r, x_s, x_r, y_s, y_r, n_s, n_r, f_s, f_r, yg_s, yg_r, xg_s, xg_r, cg_s, cg_r,
    side_s, side_r, bot_s, bot_r,
):
    place = Place()
    core, x, y, z = place.core, place.x, place.y, place.z
    partner, right, down = place.partner(), place.right(), place.down()
    peers = [place.far_z(i) for i in range(1, FAR)]
    peers += [place.along_y(i) for i in far_first(NY)]
    peers += [place.near_z(i) for i in range(NEAR - 1, 0, -1)]
    peers += [down, place.up()]
    peers += [place.along_x(i) for i in far_first(NX)]
    peers += [place.left(), right, partner]
    meet(peers)

    first = [
        send(sums.at[q, pl.ds(32 * (1 - core), 32)], core_in.at[q], core_s.at[q], core_r.at[q], partner)
        for q in COMPONENTS
    ]
    side_out = []

    def send_side(k):
        part = (slice(None), pl.ds(F + k * STEP, STEP) if k < CHUNKS else pl.ds(0, F))
        src = grad.at[part + (pl.ds(F, F),)]
        side_out.append(send(src, side.at[part], side_s.at[k], side_r.at[k], right))

    for k in range(CHUNKS):
        send_side(k)
    fetch = pltpu.make_async_copy(grad.at[:, pl.ds(0, EXT), pl.ds(0, F)], main, local_s)
    fetch.start()

    x_out, y_out, near_out, far_out = [], [], [], []
    for q, copy in zip(COMPONENTS, first):
        copy.wait_recv()
        half[q] = sums[q, pl.ds(32 * core, 32)] + core_in[q]
        out = []
        for i in far_first(NX):
            there = lax.rem(x + i, NX)
            part = half.at[q, pl.ds(NY * there, NY)]
            out.append(send(part, x_in.at[q, i - 1], x_s.at[q, i], x_r.at[q, i], place.along_x(i)))
        x_out.append(out)
    waiting = dict(zip(COMPONENTS, x_out))
    for b, bundle in enumerate(BUNDLES):
        for q in ((2,), (0, 1))[b]:
            for copy in waiting[q]:
                copy.wait_recv()
            total = half[q, pl.ds(NY * x, NY)]
            for i in range(NX - 1):
                total = total + x_in[q, i]
            x_sum[q] = total
        out = []
        for i in far_first(NY):
            there = lax.rem(y + i, NY)
            part, dst = x_sum.at[bundle, there], y_in.at[bundle, i - 1]
            out.append(send(part, dst, y_s.at[b, i], y_r.at[b, i], place.along_y(i)))
        y_out.append(out)
    send_side(CHUNKS)

    fetch.wait()
    first_col = place.col == 0
    bottom_out = []
    for k in range(CHUNKS):
        side_out[k].wait()
        rows = pl.ds(F + k * STEP, STEP)
        extra = jnp.where(first_col, 0.0, side[:, rows, :])
        bottom[:, pl.ds(k * STEP, STEP), :] = main[:, rows, :] + extra
        part = (slice(None), pl.ds(k * STEP, STEP))
        bottom_out.append(send(bottom.at[part], below.at[part], bot_s.at[k], bot_r.at[k], down))

    in_near, in_far = lax.rem(z, NEAR), lax.div(z, NEAR)
    for b, bundle in enumerate(BUNDLES):
        for copy in y_out[b]:
            copy.wait_recv()
        total = x_sum[bundle, y]
        for i in range(NY - 1):
            total = total + y_in[bundle, i]
        y_sum[bundle] = total
        near_in[bundle, in_near] = total
        out = []
        for i in range(1, NEAR):
            dst = near_in.at[bundle, in_near]
            out.append(send(y_sum.at[bundle], dst, n_s.at[b, i], n_r.at[b, i], place.near_z(i)))
        near_out.append(out)
    for b, bundle in enumerate(BUNDLES):
        for copy in near_out[b]:
            copy.wait_recv()
        total = near_in[bundle, 0]
        for i in range(1, NEAR):
            total = total + near_in[bundle, i]
        near_sum[bundle] = total
        far_in[bundle, in_far] = total
        out = []
        for i in range(1, FAR):
            dst = far_in.at[bundle, in_far]
            out.append(send(near_sum.at[bundle], dst, f_s.at[b, i], f_r.at[b, i], place.far_z(i)))
        far_out.append(out)
    for copies in far_out:
        for copy in copies:
            copy.wait_recv()
    done = far_in[:, 0]
    for i in range(1, FAR):
        done = done + far_in[:, i]
    base = 32 * core
    mine = base + NY * x + y
    home = base + NY * x
    bar = done[2] + 1.0
    tiles[home] = probe_tiles[mine] + jnp.concatenate([done[0] / bar, done[1] / bar], 0)

    yg_out = {}
    for i in far_first(NY):
        dst = tiles.at[home + SLOT_OF[NY - i]]
        yg_out[i] = send(tiles.at[home], dst, yg_s.at[i], yg_r.at[i], place.along_y(i))
    last, xg_out = [], []
    ends = [start for start, _ in GROUPS[1:]] + [NY]
    for g, (start, offsets) in enumerate(GROUPS):
        for offset in offsets:
            yg_out[NY - offset].wait_recv()
        part = tiles.at[pl.ds(home + start, ends[g] - start)]
        out = []
        for j in far_first(NX):
            out.append(send(part, part, xg_s.at[g, j], xg_r.at[g, j], place.along_x(j)))
        xg_out.append(out)
        last.append(send(part, part, cg_s.at[g, 0], cg_r.at[g, 0], partner))
    for g, (start, _) in enumerate(GROUPS):
        for j, copy in zip(far_first(NX), xg_out[g]):
            copy.wait_recv()
            there = base + NY * lax.rem(x + NX - j, NX) + start
            part = tiles.at[pl.ds(there, ends[g] - start)]
            last.append(send(part, part, cg_s.at[g, j], cg_r.at[g, j], partner))

    side_out[CHUNKS].wait()
    grad_sum[...] = main[:, pl.ds(0, F), :] + jnp.where(first_col, 0.0, side[:, pl.ds(0, F), :])
    for copy in bottom_out:
        copy.wait()
    first_row = place.row == 0
    grad_sum[:, pl.ds(0, HALO), :] += jnp.where(first_row, 0.0, below[...])
    for copies in [first, *x_out, *y_out, *near_out, *far_out, yg_out.values(), *xg_out]:
        for copy in copies:
            copy.wait_send()
    for copy in last:
        copy.wait()


def reduce_step(grad, sums, probe_tiles):
    def vmem(*shape):
        return pltpu.VMEM(shape, F32)

    return pl.pallas_call(
        reduce_kernel,
        name="reduce",
        out_shape=(
            jax.ShapeDtypeStruct((2, F, F), F32),
            jax.ShapeDtypeStruct((64, 16, HALF), F32),
        ),
        in_specs=[ANY_SPEC, VMEM_SPEC, VMEM_SPEC],
        out_specs=(VMEM_SPEC, VMEM_SPEC),
        scratch_shapes=[
            vmem(2, EXT, F),
            vmem(2, EXT, F),
            vmem(2, HALO, F),
            vmem(2, HALO, F),
            vmem(3, 32, 8, HALF),
            vmem(3, 32, 8, HALF),
            vmem(3, NX - 1, NY, 8, HALF),
            vmem(3, NY, 8, HALF),
            vmem(3, NY - 1, 8, HALF),
            vmem(3, 8, HALF),
            vmem(3, NEAR, 8, HALF),
            vmem(3, 8, HALF),
            vmem(3, FAR, 8, HALF),
            DMA,
            *[DMA((3,))] * 2,
            *[DMA((3, NX))] * 2,
            *[DMA((2, NY))] * 2,
            *[DMA((2, NEAR))] * 2,
            *[DMA((2, FAR))] * 2,
            *[DMA((NY,))] * 2,
            *[DMA((len(GROUPS), NX))] * 4,
            *[DMA((CHUNKS + 1,))] * 2,
            *[DMA((CHUNKS,))] * 2,
        ],
        compiler_params=pltpu.CompilerParams(
            collective_id=1, has_side_effects=True, vmem_limit_bytes=16 << 20
        ),
    )(grad, sums, probe_tiles)


def finish_kernel(obj, grad_sum, tiles, new_obj, new_probe):
    new_obj[...] = obj[...] + grad_sum[...]
    y = Place().y
    for there in range(NY):
        off = lax.rem(there + NY - y, NY)
        late = jnp.where(off > 4, 2 * (NY - off), 2 * off - 1)
        slot = jnp.where(off == 0, 0, late)
        for block in range(8):
            t, h = divmod(NY * block + there, 2)
            tile = tiles[NY * block + slot]
            for c in range(2):
                new_probe[c, 8 * t : 8 * t + 8, HALF * h : HALF * h + HALF] = tile[8 * c : 8 * c + 8]


def finish(obj, grad_sum, tiles):
    out = jax.ShapeDtypeStruct((2, F, F), F32)
    return pl.pallas_call(
        finish_kernel,
        name="finish",
        out_shape=(out, out),
        in_specs=[VMEM_SPEC] * 3,
        out_specs=(VMEM_SPEC, VMEM_SPEC),
        compiler_params=pltpu.CompilerParams(vmem_limit_bytes=12 << 20),
    )(obj, grad_sum, tiles)


def body(object_field, probe_field, measured, positions):
    shared = halo_exchange(object_field, probe_field, measured)
    grad, sums, probe_tiles = frame_step(positions.T, *shared)
    return finish(object_field, *reduce_step(grad, sums, probe_tiles))


def solution(mesh):
    in_specs = (P(None, "row", "col"), P(), P("row", "col", None), P("row", "col"))
    out_specs = (P(None, "row", "col"), P())
    return jax.shard_map(body, mesh=mesh, in_specs=in_specs, out_specs=out_specs, check_vma=False)
```

```python
import functools
import math

import jax
import jax.numpy as jnp
import numpy as np
from jax import lax
from jax.experimental import pallas as pl
from jax.experimental.pallas import tpu as pltpu
from jax.sharding import PartitionSpec as P

MESH = pl.DeviceIdType.MESH
DMA = pltpu.SemaphoreType.DMA
F = 256
HALF = 128
HALO = 160
EXT = F + HALO
CHUNKS = 5
TALL = F + 8
WIDE = F + 128
DEEP = EXT + 8
STEP = HALO // CHUNKS
PARTS = 10
PART = HALO // PARTS
NX, NY, NZ = 4, 8, 12
NEAR = 4
FAR = NZ // NEAR
COMPONENTS = (2, 0, 1)
BUNDLES = (pl.ds(2, 1), pl.ds(0, 2))
GROUPS = ((0, (1, 7)), (3, (2, 6)), (5, (3, 5, 4)))
SLOT_OF = (0, 1, 3, 5, 7, 6, 4, 2)
F32 = jnp.float32
BF16 = jnp.bfloat16
VMEM_SPEC = pl.BlockSpec(memory_space=pltpu.VMEM)
ANY_SPEC = pl.BlockSpec(memory_space=pl.ANY)


class Place:
    def __init__(self):
        self.row = lax.axis_index("row")
        self.col = lax.axis_index("col")
        self.rows = lax.axis_size("row")
        self.cols = lax.axis_size("col")
        self.z = lax.div(self.row, 2)
        self.x = 2 * lax.rem(self.row, 2) + lax.div(self.col, 16)
        self.y = lax.rem(lax.div(self.col, 2), NY)
        self.core = lax.rem(self.col, 2)

    def at(self, x, y, z, core):
        return (2 * z + lax.div(x, 2), 16 * lax.rem(x, 2) + 2 * y + core)

    def partner(self):
        return self.at(self.x, self.y, self.z, 1 - self.core)

    def along_x(self, i):
        return self.at(lax.rem(self.x + i, NX), self.y, self.z, self.core)

    def along_y(self, i):
        return self.at(self.x, lax.rem(self.y + i, NY), self.z, self.core)

    def near_z(self, i):
        z = NEAR * lax.div(self.z, NEAR) + lax.rem(self.z + i, NEAR)
        return self.at(self.x, self.y, z, self.core)

    def far_z(self, i):
        return self.at(self.x, self.y, lax.rem(self.z + NEAR * i, NZ), self.core)

    def up(self):
        return (lax.rem(self.row + self.rows - 1, self.rows), self.col)

    def down(self):
        return (lax.rem(self.row + 1, self.rows), self.col)

    def left(self):
        return (self.row, lax.rem(self.col + self.cols - 1, self.cols))

    def right(self):
        return (self.row, lax.rem(self.col + 1, self.cols))


def meet(devices):
    barrier = pltpu.get_barrier_semaphore()
    for device in devices:
        pl.semaphore_signal(barrier, inc=1, device_id=device, device_id_type=MESH)
    pl.semaphore_wait(barrier, len(devices))


def send(src, dst, send_sem, recv_sem, device):
    copy = pltpu.make_async_remote_copy(
        src_ref=src,
        dst_ref=dst,
        send_sem=send_sem,
        recv_sem=recv_sem,
        device_id=device,
        device_id_type=MESH,
    )
    copy.start()
    return copy


def far_first(count):
    order = []
    for d in range(count // 2, 0, -1):
        order.append(d)
        if count - d != d:
            order.append(count - d)
    return order


def halo_kernel(
    obj, probe, measured, mats, twiddle, ext, ampl, probe_out, mats_out, twiddle_out,
    raw, row_s, row_r, col_s, col_r, cor_s, cor_r, own_s,
):
    place = Place()
    up, left = place.up(), place.left()
    loads = [
        pltpu.make_async_copy(src, dst, own_s.at[i])
        for i, (src, dst) in enumerate(
            (
                (measured, raw),
                (mats, mats_out),
                (obj, ext.at[:, pl.ds(0, F), pl.ds(0, F)]),
                (probe, probe_out),
                (twiddle, twiddle_out),
            )
        )
    ]
    barrier = pltpu.get_barrier_semaphore()
    peers = (up, place.down(), left, place.right())
    for device in peers:
        pl.semaphore_signal(barrier, inc=1, device_id=device, device_id_type=MESH)
    for load in loads:
        load.start()
    pl.semaphore_wait(barrier, len(peers))
    rows = []
    for k in range(PARTS):
        here, there = pl.ds(k * PART, PART), pl.ds(F + k * PART, PART)
        dst = ext.at[:, there, pl.ds(0, F)]
        rows.append(send(obj.at[:, here], dst, row_s.at[k], row_r.at[k], up))
    side = send(obj, ext.at[:, pl.ds(0, F), pl.ds(F, F)], col_s, col_r, left)

    loads[0].wait()
    loads[1].wait()
    across, down = mats_out[4], mats_out[5]

    def reorder(f, carry):
        parts = [dot(down, part).astype(BF16) for part in split(raw[f])]
        ampl[f] = dot(parts[0], across) + dot(parts[1], across)
        return carry

    lax.fori_loop(0, raw.shape[0], reorder, 0)

    corners = []
    for k in range(PARTS):
        there = pl.ds(F + k * PART, PART)
        src, dst = ext.at[:, there, pl.ds(0, F)], ext.at[:, there, pl.ds(F, F)]
        rows[k].wait_recv()
        corners.append(send(src, dst, cor_s.at[k], cor_r.at[k], left))
    for load in loads[2:]:
        load.wait()
    side.wait()
    for k in range(PARTS):
        rows[k].wait_send()
        corners[k].wait()

    @pl.when(place.col == place.cols - 1)
    def _():
        ext[:, :, F:] = jnp.zeros((2, DEEP, F), F32)

    @pl.when(place.row == place.rows - 1)
    def _():
        ext[:, F:, :] = jnp.zeros((2, DEEP - F, 2 * F), F32)


def in_hbm(array):
    return pltpu.with_memory_space_constraint(array, pltpu.HBM)


def halo_exchange(obj, probe, measured):
    mats, twiddle = tables()
    like = jax.ShapeDtypeStruct
    frames = measured.shape[0]
    return pl.pallas_call(
        halo_kernel,
        name="halo",
        out_shape=(
            like((2, DEEP, 2 * F), F32),
            like((frames, F, F), F32),
            like((2, F, F), F32),
            like(mats.shape, BF16),
            like(twiddle.shape, F32),
        ),
        in_specs=[pl.BlockSpec(memory_space=pltpu.HBM)] * 5,
        out_specs=(VMEM_SPEC,) * 5,
        scratch_shapes=[
            pltpu.VMEM((frames, F, F), F32),
            DMA((PARTS,)),
            DMA((PARTS,)),
            DMA,
            DMA,
            DMA((PARTS,)),
            DMA((PARTS,)),
            DMA((5,)),
        ],
        compiler_params=pltpu.CompilerParams(
            collective_id=0, has_side_effects=True, vmem_limit_bytes=12 << 20
        ),
    )(*(in_hbm(a) for a in (obj, probe, measured, jnp.asarray(mats), jnp.asarray(twiddle))))


def split(x):
    high = x.astype(BF16)
    return high, (x - high.astype(F32)).astype(BF16)


def dot(a, b):
    return jnp.dot(a, b, preferred_element_type=F32)


def left_mult(high, low, x):
    x_high, x_low = split(x)
    return dot(high, x_high) + (dot(high, x_low) + dot(low, x_high))


def right_mult(x, high, low):
    x_high, x_low = split(x)
    return dot(x_high, high) + (dot(x_low, high) + dot(x_high, low))


def tables():
    k = np.arange(HALF)
    angle = 2.0 * math.pi / HALF * (np.outer(k, k) % HALF)
    cos, sin = np.cos(angle) / 16.0, np.sin(angle) / 16.0
    t1 = np.block([[cos, sin], [-sin, cos]]).astype(np.float32)
    stack = []
    for t in (t1, t1.T):
        high = t.astype(jnp.bfloat16)
        stack += [high, (t - high.astype(np.float32)).astype(jnp.bfloat16)]
    order = np.zeros((F, F), np.float32)
    for v in range(HALF):
        order[2 * v, v] = 1.0
        order[2 * v + 1, HALF + v] = 1.0
    stack += [order.astype(jnp.bfloat16), order.T.astype(jnp.bfloat16)]
    turn = 2.0 * math.pi / F * k
    down = [np.broadcast_to(f(turn)[:, None], (HALF, HALF)) for f in (np.cos, np.sin)]
    across = [np.broadcast_to(f(turn)[None, :], (8, HALF)) for f in (np.cos, np.sin)]
    twiddle = np.concatenate(down + across, 0).astype(np.float32)
    return np.stack(stack), twiddle


def frame_kernel(
    pos, ext, ampl, probe, mats, twiddle, grad, sums, probe_tiles, acc, scale
):
    grad[...] = jnp.zeros_like(grad)
    p_re, p_im = probe[0], probe[1]
    power = jnp.max(p_re * p_re + p_im * p_im, axis=0, keepdims=True)
    top = jnp.max(power, axis=1, keepdims=True)
    scale[...] = 1.0 / jnp.broadcast_to(top, scale.shape)
    for t in range(32):
        for h in range(2):
            for c in range(2):
                probe_tiles[2 * t + h, 8 * c : 8 * c + 8] = probe[
                    c, 8 * t : 8 * t + 8, HALF * h : HALF * h + HALF
                ]

    for k in range(ampl.shape[0]):
        dy, dx = pos[0, k], pos[1, k]
        r_dy, r_dx = lax.rem(dy, 8), lax.rem(dx, HALF)
        rows = pl.ds(pl.multiple_of(dy - r_dy, 8), TALL)
        lanes = pl.ds(pl.multiple_of(dx - r_dx, HALF), WIDE)
        lane = lax.broadcasted_iota(jnp.int32, (TALL, HALF), 1)
        line = lax.broadcasted_iota(jnp.int32, (32, 8, F), 1)
        back_dy, back_dx = lax.rem(8 - r_dy, 8), lax.rem(HALF - r_dx, HALF)

        def window(c):
            wide = ext[c, rows, lanes]
            turned = [pltpu.roll(wide[:, HALF * j : HALF * j + HALF], back_dx, 1) for j in range(3)]
            keep = lane < HALF - r_dx
            tall = jnp.concatenate([jnp.where(keep, turned[j], turned[j + 1]) for j in range(2)], 1)
            tall = pltpu.roll(tall.reshape(33, 8, F), back_dy, 1)
            return jnp.where(line < 8 - r_dy, tall[:32], tall[1:]).reshape(F, F)

        o_re, o_im = window(0), window(1)
        p_re, p_im = probe[0], probe[1]
        t1_high, t1_low, t2_high, t2_low = (mats[i] for i in range(4))
        down_c = jnp.concatenate([twiddle[:HALF]] * 2, 1)
        down_s = jnp.concatenate([twiddle[HALF:F]] * 2, 1)
        over_c, over_s = twiddle[F : F + 1], twiddle[F + 8 : F + 9]

        w_re = p_re * o_re - p_im * o_im
        w_im = p_re * o_im + p_im * o_re
        d_re, d_im = w_re[:HALF] - w_re[HALF:], w_im[:HALF] - w_im[HALF:]
        a = jnp.concatenate([w_re[:HALF] + w_re[HALF:], w_im[:HALF] + w_im[HALF:]], 0)
        b = jnp.concatenate([d_re * down_c + d_im * down_s, d_im * down_c - d_re * down_s], 0)
        y_even, y_odd = left_mult(t1_high, t1_low, a), left_mult(t1_high, t1_low, b)
        x_re = jnp.concatenate([y_even[:HALF], y_odd[:HALF]], 0)
        x_im = jnp.concatenate([y_even[HALF:], y_odd[HALF:]], 0)
        d_re, d_im = x_re[:, :HALF] - x_re[:, HALF:], x_im[:, :HALF] - x_im[:, HALF:]
        a = jnp.concatenate([x_re[:, :HALF] + x_re[:, HALF:], x_im[:, :HALF] + x_im[:, HALF:]], 1)
        b = jnp.concatenate([d_re * over_c + d_im * over_s, d_im * over_c - d_re * over_s], 1)

        def fit(x, target):
            re, im = x[:, :HALF], x[:, HALF:]
            factor = target * jnp.minimum(lax.rsqrt(re * re + im * im), 2.0) - 1.0
            return jnp.concatenate([re * factor, im * factor], 1)

        s_even = fit(right_mult(a, t2_high, t2_low), ampl[k, :, :HALF])
        s_odd = fit(right_mult(b, t2_high, t2_low), ampl[k, :, HALF:])
        e, o = right_mult(s_even, t1_high, t1_low), right_mult(s_odd, t1_high, t1_low)
        e_re, e_im, o_re2, o_im2 = e[:, :HALF], e[:, HALF:], o[:, :HALF], o[:, HALF:]
        q_re, q_im = o_re2 * over_c - o_im2 * over_s, o_im2 * over_c + o_re2 * over_s
        x_re = jnp.concatenate([e_re + q_re, e_re - q_re], 1)
        x_im = jnp.concatenate([e_im + q_im, e_im - q_im], 1)
        e = left_mult(t2_high, t2_low, jnp.concatenate([x_re[:HALF], x_im[:HALF]], 0))
        o = left_mult(t2_high, t2_low, jnp.concatenate([x_re[HALF:], x_im[HALF:]], 0))
        e_re, e_im, o_re2, o_im2 = e[:HALF], e[HALF:], o[:HALF], o[HALF:]
        q_re, q_im = o_re2 * down_c - o_im2 * down_s, o_im2 * down_c + o_re2 * down_s
        c_re = jnp.concatenate([e_re + q_re, e_re - q_re], 0)
        c_im = jnp.concatenate([e_im + q_im, e_im - q_im], 0)

        parts = (o_re * c_re + o_im * c_im, o_re * c_im - o_im * c_re, o_re * o_re + o_im * o_im)
        for c, part in enumerate(parts):
            acc[c] = part if k == 0 else acc[c] + part
        inverse = scale[0:1, 0:1]
        blank = jnp.zeros((1, 8, F), F32)
        edge = jnp.zeros((TALL, HALF), F32)
        below = lax.broadcasted_iota(jnp.int32, (33, 8, F), 1) >= r_dy
        beyond = lane >= r_dx
        for c, g in ((0, p_re * c_re + p_im * c_im), (1, p_re * c_im - p_im * c_re)):
            turned = pltpu.roll((g * inverse).reshape(32, 8, F), r_dy, 1)
            moved = jnp.where(
                below, jnp.concatenate([turned, blank], 0), jnp.concatenate([blank, turned], 0)
            ).reshape(TALL, F)
            first = pltpu.roll(moved[:, :HALF], r_dx, 1)
            second = pltpu.roll(moved[:, HALF:], r_dx, 1)
            grad[c, rows, lanes] += jnp.concatenate(
                [
                    jnp.where(beyond, first, edge),
                    jnp.where(beyond, second, first),
                    jnp.where(beyond, edge, second),
                ],
                1,
            )

    for t in range(32):
        for h in range(2):
            for c in range(3):
                sums[c, 2 * t + h] = acc[
                    c, 8 * t : 8 * t + 8, HALF * h : HALF * h + HALF
                ]


def frame_step(positions, ext, ampl, probe, mats, twiddle):
    return pl.pallas_call(
        frame_kernel,
        name="frames",
        out_shape=(
            jax.ShapeDtypeStruct((2, DEEP, 2 * F), F32),
            jax.ShapeDtypeStruct((3, 64, 8, HALF), F32),
            jax.ShapeDtypeStruct((64, 16, HALF), F32),
        ),
        in_specs=[
            pl.BlockSpec(memory_space=pltpu.SMEM),
            *[VMEM_SPEC] * 5,
        ],
        out_specs=(VMEM_SPEC,) * 3,
        scratch_shapes=[pltpu.VMEM((3, F, F), F32), pltpu.VMEM((8, HALF), F32)],
        compiler_params=pltpu.CompilerParams(vmem_limit_bytes=28 << 20),
    )(positions, ext, ampl, probe, mats, twiddle)


def reduce_kernel(
    grad, sums, probe_tiles, grad_sum, tiles,
    main, side, below, bottom, core_in, half, x_in, x_sum, y_in, y_sum, near_in, near_sum, far_in,
    local_s, core_s, core_r, x_s, x_r, y_s, y_r, n_s, n_r, f_s, f_r, yg_s, yg_r, xg_s, xg_r, cg_s, cg_r,
    side_s, side_r, bot_s, bot_r,
):
    place = Place()
    core, x, y, z = place.core, place.x, place.y, place.z
    partner, right, down = place.partner(), place.right(), place.down()
    peers = [place.far_z(i) for i in range(1, FAR)]
    peers += [place.along_y(i) for i in far_first(NY)]
    peers += [place.near_z(i) for i in range(NEAR - 1, 0, -1)]
    peers += [down, place.up()]
    peers += [place.along_x(i) for i in far_first(NX)]
    peers += [place.left(), right, partner]
    meet(peers)

    first = [
        send(sums.at[q, pl.ds(32 * (1 - core), 32)], core_in.at[q], core_s.at[q], core_r.at[q], partner)
        for q in COMPONENTS
    ]
    side_out = []

    def send_side(k):
        part = (slice(None), pl.ds(F + k * STEP, STEP) if k < CHUNKS else pl.ds(0, F))
        src = grad.at[part + (pl.ds(F, F),)]
        side_out.append(send(src, side.at[part], side_s.at[k], side_r.at[k], right))

    for k in range(CHUNKS):
        send_side(k)
    fetch = pltpu.make_async_copy(grad.at[:, pl.ds(0, EXT), pl.ds(0, F)], main, local_s)
    fetch.start()

    x_out, y_out, near_out, far_out = [], [], [], []
    for q, copy in zip(COMPONENTS, first):
        copy.wait_recv()
        half[q] = sums[q, pl.ds(32 * core, 32)] + core_in[q]
        out = []
        for i in far_first(NX):
            there = lax.rem(x + i, NX)
            part = half.at[q, pl.ds(NY * there, NY)]
            out.append(send(part, x_in.at[q, i - 1], x_s.at[q, i], x_r.at[q, i], place.along_x(i)))
        x_out.append(out)
    waiting = dict(zip(COMPONENTS, x_out))
    for b, bundle in enumerate(BUNDLES):
        for q in ((2,), (0, 1))[b]:
            for copy in waiting[q]:
                copy.wait_recv()
            total = half[q, pl.ds(NY * x, NY)]
            for i in range(NX - 1):
                total = total + x_in[q, i]
            x_sum[q] = total
        out = []
        for i in far_first(NY):
            there = lax.rem(y + i, NY)
            part, dst = x_sum.at[bundle, there], y_in.at[bundle, i - 1]
            out.append(send(part, dst, y_s.at[b, i], y_r.at[b, i], place.along_y(i)))
        y_out.append(out)
    send_side(CHUNKS)

    fetch.wait()
    first_col = place.col == 0
    bottom_out = []
    for k in range(CHUNKS):
        side_out[k].wait()
        rows = pl.ds(F + k * STEP, STEP)
        extra = jnp.where(first_col, 0.0, side[:, rows, :])
        bottom[:, pl.ds(k * STEP, STEP), :] = main[:, rows, :] + extra
        part = (slice(None), pl.ds(k * STEP, STEP))
        bottom_out.append(send(bottom.at[part], below.at[part], bot_s.at[k], bot_r.at[k], down))

    in_near, in_far = lax.rem(z, NEAR), lax.div(z, NEAR)
    for b, bundle in enumerate(BUNDLES):
        for copy in y_out[b]:
            copy.wait_recv()
        total = x_sum[bundle, y]
        for i in range(NY - 1):
            total = total + y_in[bundle, i]
        y_sum[bundle] = total
        near_in[bundle, in_near] = total
        out = []
        for i in range(1, NEAR):
            dst = near_in.at[bundle, in_near]
            out.append(send(y_sum.at[bundle], dst, n_s.at[b, i], n_r.at[b, i], place.near_z(i)))
        near_out.append(out)
    for b, bundle in enumerate(BUNDLES):
        for copy in near_out[b]:
            copy.wait_recv()
        total = near_in[bundle, 0]
        for i in range(1, NEAR):
            total = total + near_in[bundle, i]
        near_sum[bundle] = total
        far_in[bundle, in_far] = total
        out = []
        for i in range(1, FAR):
            dst = far_in.at[bundle, in_far]
            out.append(send(near_sum.at[bundle], dst, f_s.at[b, i], f_r.at[b, i], place.far_z(i)))
        far_out.append(out)
    for copies in far_out:
        for copy in copies:
            copy.wait_recv()
    done = far_in[:, 0]
    for i in range(1, FAR):
        done = done + far_in[:, i]
    base = 32 * core
    mine = base + NY * x + y
    home = base + NY * x
    bar = done[2] + 1.0
    tiles[home] = probe_tiles[mine] + jnp.concatenate([done[0] / bar, done[1] / bar], 0)

    yg_out = {}
    for i in far_first(NY):
        dst = tiles.at[home + SLOT_OF[NY - i]]
        yg_out[i] = send(tiles.at[home], dst, yg_s.at[i], yg_r.at[i], place.along_y(i))
    last, xg_out = [], []
    ends = [start for start, _ in GROUPS[1:]] + [NY]
    for g, (start, offsets) in enumerate(GROUPS):
        for offset in offsets:
            yg_out[NY - offset].wait_recv()
        part = tiles.at[pl.ds(home + start, ends[g] - start)]
        out = []
        for j in far_first(NX):
            out.append(send(part, part, xg_s.at[g, j], xg_r.at[g, j], place.along_x(j)))
        xg_out.append(out)
        last.append(send(part, part, cg_s.at[g, 0], cg_r.at[g, 0], partner))
    for g, (start, _) in enumerate(GROUPS):
        for j, copy in zip(far_first(NX), xg_out[g]):
            copy.wait_recv()
            there = base + NY * lax.rem(x + NX - j, NX) + start
            part = tiles.at[pl.ds(there, ends[g] - start)]
            last.append(send(part, part, cg_s.at[g, j], cg_r.at[g, j], partner))

    side_out[CHUNKS].wait()
    grad_sum[...] = main[:, pl.ds(0, F), :] + jnp.where(first_col, 0.0, side[:, pl.ds(0, F), :])
    for copy in bottom_out:
        copy.wait()
    first_row = place.row == 0
    grad_sum[:, pl.ds(0, HALO), :] += jnp.where(first_row, 0.0, below[...])
    for copies in [first, *x_out, *y_out, *near_out, *far_out, yg_out.values(), *xg_out]:
        for copy in copies:
            copy.wait_send()
    for copy in last:
        copy.wait()


def reduce_step(grad, sums, probe_tiles):
    def vmem(*shape):
        return pltpu.VMEM(shape, F32)

    return pl.pallas_call(
        reduce_kernel,
        name="reduce",
        out_shape=(
            jax.ShapeDtypeStruct((2, F, F), F32),
            jax.ShapeDtypeStruct((64, 16, HALF), F32),
        ),
        in_specs=[ANY_SPEC, VMEM_SPEC, VMEM_SPEC],
        out_specs=(VMEM_SPEC, VMEM_SPEC),
        scratch_shapes=[
            vmem(2, EXT, F),
            vmem(2, EXT, F),
            vmem(2, HALO, F),
            vmem(2, HALO, F),
            vmem(3, 32, 8, HALF),
            vmem(3, 32, 8, HALF),
            vmem(3, NX - 1, NY, 8, HALF),
            vmem(3, NY, 8, HALF),
            vmem(3, NY - 1, 8, HALF),
            vmem(3, 8, HALF),
            vmem(3, NEAR, 8, HALF),
            vmem(3, 8, HALF),
            vmem(3, FAR, 8, HALF),
            DMA,
            *[DMA((3,))] * 2,
            *[DMA((3, NX))] * 2,
            *[DMA((2, NY))] * 2,
            *[DMA((2, NEAR))] * 2,
            *[DMA((2, FAR))] * 2,
            *[DMA((NY,))] * 2,
            *[DMA((len(GROUPS), NX))] * 4,
            *[DMA((CHUNKS + 1,))] * 2,
            *[DMA((CHUNKS,))] * 2,
        ],
        compiler_params=pltpu.CompilerParams(
            collective_id=1, has_side_effects=True, vmem_limit_bytes=16 << 20
        ),
    )(grad, sums, probe_tiles)


def finish_kernel(obj, grad_sum, tiles, new_obj, new_probe):
    new_obj[...] = obj[...] + grad_sum[...]
    y = Place().y
    for there in range(NY):
        off = lax.rem(there + NY - y, NY)
        late = jnp.where(off > 4, 2 * (NY - off), 2 * off - 1)
        slot = jnp.where(off == 0, 0, late)
        for block in range(8):
            t, h = divmod(NY * block + there, 2)
            tile = tiles[NY * block + slot]
            for c in range(2):
                new_probe[c, 8 * t : 8 * t + 8, HALF * h : HALF * h + HALF] = tile[8 * c : 8 * c + 8]


def finish(obj, grad_sum, tiles):
    out = jax.ShapeDtypeStruct((2, F, F), F32)
    return pl.pallas_call(
        finish_kernel,
        name="finish",
        out_shape=(out, out),
        in_specs=[VMEM_SPEC] * 3,
        out_specs=(VMEM_SPEC, VMEM_SPEC),
        compiler_params=pltpu.CompilerParams(vmem_limit_bytes=12 << 20),
    )(obj, grad_sum, tiles)


def body(object_field, probe_field, measured, positions):
    shared = halo_exchange(object_field, probe_field, measured)
    grad, sums, probe_tiles = frame_step(positions.T, *shared)
    return finish(object_field, *reduce_step(grad, sums, probe_tiles))


def solution(mesh):
    in_specs = (P(None, "row", "col"), P(), P("row", "col", None), P("row", "col"))
    out_specs = (P(None, "row", "col"), P())
    return jax.shard_map(body, mesh=mesh, in_specs=in_specs, out_specs=out_specs, check_vma=False)
```
